512 devices in a mesh: fx: 8 (over y_lo, x), fy: 16 (over z), fz: 4 (over y_hi, core).
Axes of the slice: x: 4, y: 4 (y_hi: 2, y_lo: 2; y = y_hi * 2 + y_lo), z: 16, core: 2. Of those that a mesh axis runs over, the one named last changes fastest.
Arguments:
- density: float32 [64, 128, 512], P('fx', 'fy', 'fz'), may hold values from 0.8 to 1.25
- velocity: float32 [3, 64, 128, 512], P(None, 'fx', 'fy', 'fz'), may hold values from -2 to 2
- pressure: float32 [64, 128, 512], P('fx', 'fy', 'fz'), may hold values from 0.7 to 1.4
- acoustic: float32 [8192, 4, 512], P(('fx', 'fy', 'fz')), may hold values from -6 to 6
- sound_speed: float32 [8192], P(('fx', 'fy', 'fz')), may hold values from 0.5 to 2
- derivative: float32 [8, 8], replicated, may hold values from -2 to 2
- mode_basis: float32 [8, 8], replicated, may hold values from -2 to 2
- neighbours: int32 [8192, 6], P(('fx', 'fy', 'fz')), may hold values from 0 to 8191, as said below
- block_owner: int32 [8, 16, 4, 16, 1], P('fx', 'fy', 'fz'), may hold values from 0 to 15; in each aligned block of 16 rows (0 to 15, 16 to 31, ..., all dimensions but the last counted through in order) at most 2 rows name the same one
- block_element: int32 [8, 16, 4, 16], P('fx', 'fy', 'fz'), may hold values from 0 to 15
Outputs:
- flow_state: float32 [5, 64, 128, 512], P(None, 'fx', 'fy', 'fz')
- sound_state: float32 [8192, 4, 512], P(('fx', 'fy', 'fz'))
The draws below stay inside these ranges and needn't reach their ends.
Inputs may be any that keep to these rules, and one draw needn't show every extreme that they name: `neighbours`: across faces -x, -y, -z the neighbour of element e lies in e - 16 to e, across faces +x, +y, +z in e to e + 16. `block_owner`: the 16 blocks of one flow device name one fy index at most 2 times.
All inputs are finite; a program needn't handle non-finite values.
Results may differ from the reference program's by a relative error of at most 0.0001.
Values sent between devices are 32-bit elements; how exact they have to be, the bound alone decides.
A program may use at most 64 MiB of HBM per device.

```python
import math
import jax
import jax.numpy as jnp
import numpy as np
from jax import lax

CX = 8
CY = 8
CZ = 128
NODES = 512
NX = 64
NY = 128
NZ = 512
BLK_DEV = 16
EL_DEV = 16
ELEMS = 8192
CAP = 2
N_FX = 8
N_FY = 16
N_FZ = 4


def draw_neighbours(key, part):
    downward = jax.random.randint(jax.random.fold_in(key, 11), (ELEMS, 6), -EL_DEV, 1)
    upward = jax.random.randint(jax.random.fold_in(key, 12), (ELEMS, 6), 0, EL_DEV + 1)
    face_index = jnp.arange(6, dtype=jnp.int32)[None, :]
    is_lower = face_index % 2 == 0
    offsets = jnp.where(is_lower, downward, upward)
    element_index = jnp.arange(ELEMS, dtype=jnp.int32)[:, None]
    second = (element_index >= EL_DEV) & (element_index < 2 * EL_DEV)
    offsets = jnp.where(second, jnp.where(is_lower, -EL_DEV, EL_DEV), offsets)
    forced = (element_index % EL_DEV == 0) & (face_index == 1)
    offsets = jnp.where(forced, EL_DEV, offsets)
    return jnp.clip(element_index + offsets, 0, ELEMS - 1).astype(jnp.int32)


def plant(result, own_key, low, high):
    dims = result.shape
    spot = [jax.random.randint(jax.random.fold_in(own_key, axis), (), 0, dims[axis]) for axis in range(len(dims))]
    result = result.at[tuple(spot)].set(low)
    longest = dims.index(max(dims))
    spot[longest] = (spot[longest] + 1) % dims[longest]
    return result.at[tuple(spot)].set(high)


def block_levels(rng, extent, split, smallest, largest):
    def one(position, parts):
        heights = jax.random.uniform(jax.random.fold_in(jax.random.fold_in(rng, 6), position), (parts,), jnp.float32, smallest / len(split), largest / len(split))
        return jnp.repeat(jnp.exp(heights), extent[position] // parts).reshape((-1,) + (1,) * (len(extent) - position - 1))

    gain = one(*split[0])
    for cut in split[1:]:
        gain = gain * one(*cut)
    return gain


def deal_out(key, own, number, rows, number_of, top, most, skew):
    ranking = jax.random.permutation(key, number_of)
    packed, ordinary = portions_of(number_of, rows * top, most, skew, True), portions_of(number_of, rows * top, most, skew, False)
    places = jnp.arange(number_of)

    def named(lengths, rotation):
        used = int((lengths > 0).sum())
        fixed = max(1, used // 4)
        shifted = fixed + (places - fixed + rotation * (used - fixed)) % max(1, number_of - fixed)
        return jnp.zeros((number_of,), jnp.int32).at[ranking[jnp.where(places < fixed, places, shifted)]].set(jnp.asarray(lengths, jnp.int32))

    lengths = jnp.where(number % 4 == 0, named(packed, number // 4), named(ordinary, number - number // 4 - 1))
    mixed = jax.random.permutation(jax.random.fold_in(own, 3), number_of)
    donor, sink = mixed[0:number_of // 2 * 2:2], mixed[1:number_of // 2 * 2:2]
    margin = jnp.minimum(lengths[donor] - 1, most - lengths[sink]) // 2
    margin = jnp.where((donor == ranking[0]) | (sink == ranking[0]) | (lengths[sink] == 0), 0, jnp.maximum(margin, 0))
    shifted = jax.random.randint(jax.random.fold_in(own, 4), (number_of // 2,), 0, 1 << 20) % (margin + 1)
    lengths = lengths.at[donor].add(-shifted).at[sink].add(shifted)
    members = jnp.searchsorted(jnp.cumsum(lengths), jnp.arange(rows * top), side="right").astype(jnp.int32)
    table = members.reshape(top, rows).T
    table = table[jax.random.permutation(jax.random.fold_in(own, 1), rows)]
    rotation = jax.random.randint(jax.random.fold_in(own, 2), (rows, 1), 0, top)
    return jnp.take_along_axis(table, (jnp.arange(top)[None, :] + rotation) % top, axis=1)


def portions_of(count, total, bound, skew, full):
    portions = [(1 << 20) // math.isqrt(grade ** skew) + 1 for grade in range(1, count + 1)]
    largest = bound if full else min(bound, max(-(-total // count), total * portions[0] // sum(portions)))
    least = 1 if total - largest >= count - 1 else 0
    counts, spare = [largest] + [least] * (count - 1), total - largest - least * (count - 1)
    while spare > 0:
        free = [i for i in range(1, count) if counts[i] < largest] or [i for i in range(1, count) if counts[i] < bound]
        pool, remaining = sum([portions[i] for i in free]), spare
        for i in free:
            addition = min(bound - counts[i], max(1, remaining * portions[i] // pool), spare)
            counts[i] = counts[i] + addition
            spare = spare - addition
    return np.array(counts)


def centred(rng, extent, spread, bound, cuts=(), kind=jnp.bfloat16):
    gain = block_levels(rng, extent, cuts, -0.22, 0.18) if cuts else 1.0
    result = jax.random.normal(rng, extent, jnp.float32) * spread * gain
    return jnp.minimum(jnp.maximum(result, -bound), bound).astype(kind)


def setup_inputs(seed: int = 0) -> dict:
    arg_keys = jax.random.split(jax.random.key(seed), 11)
    density = jnp.clip(jnp.exp(math.log(1.25) - 0.4462871 * jax.random.uniform(arg_keys[0], (NX, NY, NZ), jnp.float32) ** block_levels(arg_keys[0], (NX, NY, NZ), ((0, 8), (1, 16), (2, 4)), -0.2, 0.2)), 0.8, 1.25)
    velocity = centred(arg_keys[1], (3, NX, NY, NZ), 0.5, 2.0, ((1, 8), (2, 16), (3, 4)), jnp.float32)
    pressure = jnp.clip(jnp.exp(math.log(1.4) - 0.6931472 * jax.random.uniform(arg_keys[2], (NX, NY, NZ), jnp.float32) ** block_levels(arg_keys[2], (NX, NY, NZ), ((0, 8), (1, 16), (2, 4)), -0.2, 0.2)), 0.7, 1.4)
    acoustic = centred(arg_keys[3], (ELEMS, 4, NODES), 1.0, 6.0, ((0, 512),), jnp.float32)
    sound_speed = jnp.clip(jnp.exp(math.log(2.0) - 1.3862944 * jax.random.uniform(arg_keys[4], (ELEMS,), jnp.float32) ** block_levels(arg_keys[4], (ELEMS,), ((0, 512),), -0.2, 0.2)), 0.5, 2.0)
    derivative = centred(arg_keys[5], (8, 8), 8 ** -0.5, 2.0, (), jnp.float32)
    mode_basis = centred(arg_keys[6], (8, 8), 8 ** -0.5, 2.0, (), jnp.float32)
    neighbours = draw_neighbours(jax.random.fold_in(arg_keys[10], 71), 0)
    block_owner_keys = jax.random.split(jax.random.fold_in(arg_keys[8], 1), N_FX * N_FY * N_FZ * BLK_DEV // BLK_DEV)
    block_owner_turns = jax.random.permutation(jax.random.fold_in(arg_keys[8], 3), N_FX * N_FY * N_FZ * BLK_DEV // BLK_DEV)
    block_owner = jax.vmap(lambda own, number: deal_out(jax.random.fold_in(arg_keys[8], 2), own, number, BLK_DEV, N_FY, 1, CAP, 2))(block_owner_keys, block_owner_turns).reshape((N_FX, N_FY, N_FZ, BLK_DEV, 1))
    block_element = plant(jax.random.randint(arg_keys[9], (N_FX, N_FY, N_FZ, BLK_DEV), 0, EL_DEV), jax.random.fold_in(arg_keys[9], 1), 0, EL_DEV - 1).astype(jnp.int32)
    return dict(density=density, velocity=velocity, pressure=pressure, acoustic=acoustic, sound_speed=sound_speed, derivative=derivative, mode_basis=mode_basis, neighbours=neighbours, block_owner=block_owner, block_element=block_element)


HEAT_RATIO = 1.4
TIME_STEP = 0.1
VISCOSITY = 0.05
PENALTY = 0.5
HIGHEST = lax.Precision.HIGHEST

def cut_range(values, along, start_at, stop_at):
    return lax.slice_in_dim(values, start_at, stop_at, axis=along + 1)

def interior(padded, along):
    for other in range(3):
        if other != along:
            padded = cut_range(padded, other, 1, padded.shape[other + 1] - 1)
    return padded

def flow_section(padded):
    center = padded[:, 1:-1, 1:-1, 1:-1]
    velocity_mid = center[1:4] / center[0]
    flow_rate = jnp.zeros_like(center)
    laplace = jnp.zeros_like(velocity_mid)
    slopes = []
    for along in range(3):
        stripe = interior(padded, along)
        length = stripe.shape[along + 1]
        velocity_cells = stripe[1:4] / stripe[0]
        pressure_cells = (HEAT_RATIO - 1.0) * (stripe[4] - 0.5 * lax.optimization_barrier(jnp.sum(stripe[1:4] * velocity_cells, 0)))
        signal_speed = (jnp.abs(velocity_cells[along]) + jnp.sqrt(HEAT_RATIO * jnp.abs(pressure_cells) / stripe[0]))[None]
        unit_axis = (jnp.arange(3) == along).astype(jnp.float32)
        momentum_flux = stripe[1:4] * velocity_cells[along] + unit_axis[:, None, None, None] * pressure_cells
        fluxes = jnp.concatenate([stripe[1 + along][None], momentum_flux, ((stripe[4] + pressure_cells) * velocity_cells[along])[None]], 0)
        wave_speed = jnp.maximum(cut_range(signal_speed, along, 0, length - 1), cut_range(signal_speed, along, 1, length))
        face_flux = 0.5 * (cut_range(fluxes, along, 0, length - 1) + cut_range(fluxes, along, 1, length)) - 0.5 * wave_speed * (cut_range(stripe, along, 1, length) - cut_range(stripe, along, 0, length - 1))
        flow_rate = flow_rate - (cut_range(face_flux, along, 1, length - 1) - cut_range(face_flux, along, 0, length - 2))
        laplace = laplace + cut_range(stripe[1:4], along, 2, length) + cut_range(stripe[1:4], along, 0, length - 2) - 2.0 * center[1:4]
        slopes.append(0.5 * (cut_range(velocity_cells, along, 2, length) - cut_range(velocity_cells, along, 0, length - 2)))
    empty_row = jnp.zeros_like(center[:1])
    flow_rate = flow_rate + VISCOSITY * jnp.concatenate([empty_row, laplace, empty_row], 0)
    vorticity = jnp.stack([slopes[1][2] - slopes[2][1], slopes[2][0] - slopes[0][2], slopes[0][1] - slopes[1][0]])
    lamb_vector = jnp.stack([vorticity[1] * velocity_mid[2] - vorticity[2] * velocity_mid[1], vorticity[2] * velocity_mid[0] - vorticity[0] * velocity_mid[2], vorticity[0] * velocity_mid[1] - vorticity[1] * velocity_mid[0]])
    return (flow_rate, lamb_vector)

def conserved(density, velocity, pressure):
    energy = pressure / (HEAT_RATIO - 1.0) + 0.5 * density * lax.optimization_barrier(jnp.sum(velocity * velocity, 0))
    return jnp.concatenate([density[None], density[None] * velocity, energy[None]], 0)

def face_columns():
    node_grid = np.arange(512).reshape(8, 8, 8)
    surfaces = [node_grid[0], node_grid[7], node_grid[:, 0], node_grid[:, 7], node_grid[:, :, 0], node_grid[:, :, 7]]
    columns = np.concatenate([surface.reshape(64) for surface in surfaces])
    chooser = np.zeros((512, 384))
    chooser[columns, np.arange(384)] = 1.0
    return jnp.asarray(chooser, jnp.float32)

def kron_cube(basis_one):
    return jnp.kron(basis_one, jnp.kron(basis_one, basis_one))

def derivative_tables(derivative):
    identity = jnp.eye(8, dtype=jnp.float32)
    along_x = jnp.kron(derivative.T, jnp.kron(identity, identity))
    along_y = jnp.kron(identity, jnp.kron(derivative.T, identity))
    along_z = jnp.kron(identity, jnp.kron(identity, derivative.T))
    return (jnp.concatenate([along_x, along_y, along_z], 1), jnp.concatenate([along_x, along_y, along_z], 0))

def extract(state_now, chooser):
    return jnp.dot(state_now.reshape(-1, 512), chooser, precision=HIGHEST).reshape(state_now.shape[0], 4, 384)

def face_jumps(own_faces, face_table, neighbour_rows):
    pieces = []
    for facet_index in range(6):
        opposite = facet_index ^ 1
        remote = face_table[:, :, opposite * 64:(opposite + 1) * 64][neighbour_rows[:, facet_index]]
        pieces.append(remote - own_faces[:, :, facet_index * 64:(facet_index + 1) * 64])
    return jnp.concatenate(pieces, 2)

def acoustic_rate(state_now, jumps, source, sound_speed, grad_table, div_table, chooser):
    element_count = state_now.shape[0]
    pressure_gradient = jnp.dot(state_now[:, 0], grad_table, precision=HIGHEST).reshape(element_count, 3, 512)
    divergence = jnp.dot(state_now[:, 1:4].reshape(element_count, 1536), div_table, precision=HIGHEST)
    lifted = jnp.dot(jumps.reshape(element_count * 4, 384), chooser.T, precision=HIGHEST).reshape(element_count, 4, 512)
    rate_pressure = -(sound_speed * sound_speed)[:, None] * divergence + PENALTY * lifted[:, 0]
    rate_velocity = -pressure_gradient + source + PENALTY * lifted[:, 1:4]
    return jnp.concatenate([rate_pressure[:, None], rate_velocity], 1)

def reference(density, velocity, pressure, acoustic, sound_speed, derivative, mode_basis, neighbours, block_owner, block_element):
    grad_table, div_table = derivative_tables(derivative)
    chooser = face_columns()
    basis = kron_cube(mode_basis)
    fx_index = jnp.arange(N_FX, dtype=jnp.int32)[:, None, None, None]
    fz_index = jnp.arange(N_FZ, dtype=jnp.int32)[None, None, :, None]
    element_ids = (((fx_index * N_FY + block_owner[..., 0]) * N_FZ + fz_index) * EL_DEV + block_element).reshape(-1).astype(jnp.int32)

    def section(flow_now, sound_now):
        padded = jnp.pad(flow_now, ((0, 0), (1, 1), (1, 1), (1, 1)), mode='wrap')
        flow_rate, lamb_vector = flow_section(padded)
        blocks = lamb_vector.reshape(3, N_FX, CX // 8, 8, N_FY, CY // 8, 8, N_FZ, CZ // 8, 8)
        blocks = blocks.transpose(1, 4, 7, 2, 5, 8, 0, 3, 6, 9).reshape(-1, 512)
        projected = jnp.dot(blocks, basis.T, precision=HIGHEST).reshape(-1, 1536)
        source = jax.ops.segment_sum(projected, element_ids, num_segments=ELEMS).reshape(ELEMS, 3, 512)
        own_faces = extract(sound_now, chooser)
        jumps = face_jumps(own_faces, own_faces, neighbours)
        return (flow_rate, acoustic_rate(sound_now, jumps, source, sound_speed, grad_table, div_table, chooser))
    flow_start = conserved(density, velocity, pressure)
    sound_start = acoustic
    rate_one, sound_rate = section(flow_start, sound_start)
    flow_one = flow_start + TIME_STEP * rate_one
    sound_one = sound_start + TIME_STEP * sound_rate
    rate_two, sound_rate = section(flow_one, sound_one)
    flow_two = 0.75 * flow_start + 0.25 * (flow_one + TIME_STEP * rate_two)
    sound_two = 0.75 * sound_start + 0.25 * (sound_one + TIME_STEP * sound_rate)
    rate_three, sound_rate = section(flow_two, sound_two)
    flow_state = 1.0 / 3.0 * flow_start + 2.0 / 3.0 * (flow_two + TIME_STEP * rate_three)
    sound_state = 1.0 / 3.0 * sound_start + 2.0 / 3.0 * (sound_two + TIME_STEP * sound_rate)
    return (flow_state, sound_state)
```

```python
import functools

import jax
import jax.numpy as jnp
from jax import lax
from jax.experimental import pallas as pl
from jax.experimental.pallas import tpu as pltpu
from jax.sharding import PartitionSpec as P

HEAT_RATIO = 1.4
TIME_STEP = 0.1
VISCOSITY = 0.05
PENALTY = 0.5
HIGHEST = lax.Precision.HIGHEST
MESH = pl.DeviceIdType.MESH
BLEND = ((0.0, 1.0), (0.75, 0.25), (1.0 / 3.0, 2.0 / 3.0))
F32 = jnp.float32
BF16 = jnp.bfloat16


def dot(a, b):
    return jnp.dot(a, b, precision=HIGHEST, preferred_element_type=F32)


def dot_nt(a, b):
    return lax.dot_general(
        a, b, (((1,), (1,)), ((), ())), precision=HIGHEST, preferred_element_type=F32
    )


def dot_tn(a, b):
    return lax.dot_general(
        a, b, (((0,), (0,)), ((), ())), precision=HIGHEST, preferred_element_type=F32
    )


def pick(values, chooser):
    rows = values.shape[0]
    high = values.astype(BF16)
    rest = values - high.astype(F32)
    middle = rest.astype(BF16)
    low = (rest - middle.astype(F32)).astype(BF16)
    parts = jnp.dot(
        jnp.concatenate([high, middle, low], 0), chooser, preferred_element_type=F32
    )
    return parts[:rows] + parts[rows : 2 * rows] + parts[2 * rows :]


def iota(shape, dim):
    return lax.broadcasted_iota(jnp.int32, shape, dim)


def eighth(values):
    return lax.shift_right_logical(values, 3)


def repeat_rows(matrix, count, by_block, turned=False):
    rows, columns = iota((count, 8), 0), iota((count, 8), 1)
    chooser = ((eighth(rows) if by_block else rows & 7) == columns).astype(F32)
    if turned:
        return dot_nt(chooser, dot(chooser, matrix))
    return dot_nt(dot(chooser, matrix), chooser)


def swap_groups(values):
    rows, groups = iota((16, 128), 0), eighth(iota((16, 128), 1))
    for bit in range(4):
        step = 1 << bit
        row_bit, group_bit = (rows & step) != 0, (groups & step) != 0
        down = pltpu.roll(pltpu.roll(values, 16 - step, 1), 8 * step, 2)
        up = pltpu.roll(pltpu.roll(values, step, 1), 128 - 8 * step, 2)
        values = jnp.where(
            (row_bit == group_bit)[None], values, jnp.where(group_bit[None], down, up)
        )
    return values


def sweep(cells, along):
    density, momentum, energy = cells[0], cells[1:4], cells[4]
    inverse = 1.0 / density
    velocity = [part * inverse for part in momentum]
    kinetic = sum(part * speed for part, speed in zip(momentum, velocity))
    pressure = (HEAT_RATIO - 1.0) * (energy - 0.5 * kinetic)
    normal = velocity[along]
    signal = jnp.abs(normal) + jnp.sqrt(HEAT_RATIO * jnp.abs(pressure) * inverse)
    half_speed = 0.5 * jnp.maximum(signal[:-1], signal[1:])
    fluxes = [momentum[along]] + [part * normal for part in momentum] + [(energy + pressure) * normal]
    fluxes[1 + along] = fluxes[1 + along] + pressure
    rates = []
    for index, (flux, cell) in enumerate(zip(fluxes, cells)):
        gap = cell[1:] - cell[:-1]
        face = 0.5 * (flux[:-1] + flux[1:]) - half_speed * gap
        rate = face[:-1] - face[1:]
        if 1 <= index <= 3:
            rate = rate + VISCOSITY * (gap[1:] - gap[:-1])
        rates.append(rate)
    slopes = [0.5 * (velocity[c][2:] - velocity[c][:-2]) for c in range(3) if c != along]
    return rates + slopes


def kernel(
    sizes,
    density_ref,
    velocity_ref,
    pressure_ref,
    acoustic_ref,
    speed_ref,
    derivative_ref,
    basis_ref,
    neighbour_ref,
    owner_ref,
    element_ref,
    flow_out,
    sound_out,
    flow,
    halo_send,
    halo_recv,
    turned,
    sound,
    trace,
    trace_recv,
    rate_ref,
    packed,
    arrived,
    labels,
    labels_recv,
    gather_ref,
    place_ref,
    route_ref,
    pair_ref,
    slope_ref,
    slope_z_ref,
    halo_out_sem,
    halo_in_sem,
    trace_out_sem,
    trace_in_sem,
    packed_out_sem,
    packed_in_sem,
    label_out_sem,
    label_in_sem,
):
    n_x, n_y, n_z = sizes
    fx, fy, fz = lax.axis_index("fx"), lax.axis_index("fy"), lax.axis_index("fz")
    place = (fx * n_y + fy) * n_z + fz
    total = n_x * n_y * n_z

    def device_at(index):
        return (index // (n_y * n_z), (index // n_z) % n_y, index % n_z)

    after, before = device_at((place + 1) % total), device_at((place + total - 1) % total)
    beside = [
        ((fx + 1) % n_x, fy, fz),
        ((fx + n_x - 1) % n_x, fy, fz),
        (fx, (fy + 1) % n_y, fz),
        (fx, (fy + n_y - 1) % n_y, fz),
        (fx, fy, (fz + 1) % n_z),
        (fx, fy, (fz + n_z - 1) % n_z),
    ]
    barrier = pltpu.get_barrier_semaphore()
    for device in [beside[0], beside[1], beside[4], beside[5], after, before]:
        pl.semaphore_signal(barrier, inc=1, device_id=device, device_id_type=MESH)

    @pl.loop(1, n_y)
    def _(step):
        pl.semaphore_signal(
            barrier, inc=1, device_id=(fx, (fy + step) % n_y, fz), device_id_type=MESH
        )

    lane = iota((8, 128), 1)
    digit = lane & 7

    def pack_halos(stage):
        for side, row in ((0, 7), (1, 0)):
            halo_send[stage, side] = flow[stage, :, pl.ds(row, 8, stride=8), :]
        ends = [jnp.zeros((5, 8, 128), F32)] * 2
        for x in range(8):
            plane = flow[stage, :, 8 * x : 8 * x + 8, :]
            ends[0] = jnp.where(lane == x, pltpu.roll(plane, x + 1, 2), ends[0])
            ends[1] = jnp.where(lane == x, pltpu.roll(plane, x, 2) if x else plane, ends[1])
        halo_send[stage, 2], halo_send[stage, 3] = ends

    def halo_copies(stage):
        sources = [flow.at[stage, :, pl.ds(56, 8), :], flow.at[stage, :, pl.ds(0, 8), :]]
        sources += [halo_send.at[stage, index] for index in range(4)]
        return [
            pltpu.make_async_remote_copy(
                src_ref=source,
                dst_ref=halo_recv.at[stage, index],
                send_sem=halo_out_sem.at[stage, index],
                recv_sem=halo_in_sem.at[stage, index],
                device_id=beside[index],
                device_id_type=MESH,
            )
            for index, source in enumerate(sources)
        ]

    def take_traces(stage):
        trace[stage, 0, 0] = sound[stage, :, 0:8, :]
        trace[stage, 1, 0] = sound[stage, :, 56:64, :]
        trace[stage, 0, 1] = sound[stage, :, pl.ds(0, 8, stride=8), :]
        trace[stage, 1, 1] = sound[stage, :, pl.ds(7, 8, stride=8), :]
        ends = [jnp.zeros((4, 8, 128), F32)] * 2
        for x in range(8):
            plane = sound[stage, :, 8 * x : 8 * x + 8, :]
            ends[0] = jnp.where(digit == x, pltpu.roll(plane, x, 2) if x else plane, ends[0])
            ends[1] = jnp.where(digit == x, pltpu.roll(plane, 121 + x, 2) if x < 7 else plane, ends[1])
        trace[stage, 0, 2], trace[stage, 1, 2] = ends

    def trace_copies(stage):
        return [
            pltpu.make_async_remote_copy(
                src_ref=trace.at[stage, 1 - side],
                dst_ref=trace_recv.at[stage, side],
                send_sem=trace_out_sem.at[stage, side],
                recv_sem=trace_in_sem.at[stage, side],
                device_id=device,
                device_id_type=MESH,
            )
            for side, device in ((0, after), (1, before))
        ]

    def spread(source, target, out_sem, in_sem):
        @pl.loop(1, n_y)
        def _(step):
            peer = (fy + step) % n_y
            pltpu.make_async_remote_copy(
                src_ref=source.at[peer],
                dst_ref=target.at[fy],
                send_sem=out_sem,
                recv_sem=in_sem,
                device_id=(fx, peer, fz),
                device_id_type=MESH,
            ).start()

        target[fy] = source[fy]

    def spread_whole(source, target, out_sem, in_sem):
        return pltpu.make_async_remote_copy(
            src_ref=source.at[pl.ds(0, n_y - 1)],
            dst_ref=target.at[pl.ds(0, n_y - 1)],
            send_sem=out_sem,
            recv_sem=in_sem,
            device_id=beside[2],
            device_id_type=MESH,
        )

    def label_args():
        return (labels, labels_recv, label_out_sem.at[0], label_in_sem.at[0])

    def packet_args(stage):
        return (
            packed.at[stage],
            arrived.at[stage],
            packed_out_sem.at[stage],
            packed_in_sem.at[stage],
        )

    density = density_ref[...].reshape(64, 128)
    speeds = velocity_ref[...].reshape(3, 64, 128)
    energy = pressure_ref[...].reshape(64, 128) / (HEAT_RATIO - 1.0) + 0.5 * density * (
        speeds[0] * speeds[0] + speeds[1] * speeds[1] + speeds[2] * speeds[2]
    )
    flow[0, 0] = density
    for part in range(3):
        flow[0, 1 + part] = density * speeds[part]
    flow[0, 4] = energy
    pack_halos(0)

    pl.semaphore_wait(barrier, 6 + n_y - 1)
    halos = [halo_copies(0)]
    for copy in halos[0]:
        copy.start()

    nodes = jnp.stack(
        [
            acoustic_ref[:, field, 128 * part : 128 * part + 128]
            for field in range(4)
            for part in range(4)
        ],
        0,
    )
    sound[0] = swap_groups(nodes).reshape(4, 64, 128)
    take_traces(0)
    traces = [trace_copies(0)]
    for copy in traces[0]:
        copy.start()

    widen = (iota((16, 128), 0) == eighth(iota((16, 128), 1))).astype(F32)
    owner = dot(owner_ref[...].astype(F32), widen)
    element = dot(element_ref[...].astype(F32), widen)
    rows_out = 8 * n_y
    row, column = iota((rows_out, 128), 0), iota((rows_out, 128), 1)
    same_digit = (row & 7) == (column & 7)
    earlier = (
        (eighth(iota((128, 128), 0)) < eighth(iota((128, 128), 1)))
        & ((iota((128, 128), 0) & 7) == 0)
    ).astype(F32)
    named = owner.astype(jnp.int32) == eighth(row)
    count = jnp.dot(named.astype(BF16), earlier.astype(BF16), preferred_element_type=F32)
    first, second = named & (count < 0.5), named & (count > 0.5)
    mark = jnp.where((column & 7) == 0, element + 1.0, 0.0)
    label = jnp.where(
        column < 64,
        jnp.sum(jnp.where(first, mark, 0.0), 1, keepdims=True),
        jnp.sum(jnp.where(second, mark, 0.0), 1, keepdims=True),
    )
    labels[...] = label.reshape(n_y, 8, 128)
    spread(*label_args())

    basis = basis_ref[...]
    tiled = repeat_rows(basis, 128, False)[:rows_out]
    route_ref[:, 0:128] = jnp.where(first, tiled, 0.0)
    route_ref[:, 128:256] = jnp.where(second, tiled, 0.0)
    pair_ref[...] = repeat_rows(basis, 64, True) * repeat_rows(basis, 64, False)

    derivative = derivative_ref[...]
    row64, column64 = iota((64, 64), 0), iota((64, 64), 1)
    slope_ref[0:64, :] = jnp.where(
        (row64 & 7) == (column64 & 7), repeat_rows(derivative, 64, True), 0.0
    )
    slope_ref[64:128, :] = jnp.where(
        eighth(row64) == eighth(column64), repeat_rows(derivative, 64, False), 0.0
    )
    row128, column128 = iota((128, 128), 0), iota((128, 128), 1)
    slope_z_ref[...] = jnp.where(
        eighth(row128) == eighth(column128), repeat_rows(derivative, 128, False, True), 0.0
    )

    local = (neighbour_ref[...] - place * 16).astype(F32)
    nearby = dot_tn(local, widen).astype(jnp.int32)
    row256, column256 = iota((256, 128), 0), iota((256, 128), 1)
    matching = (row256 & 7) == (column256 & 7)
    for face in range(6):
        index = nearby[face : face + 1] + (16 if face % 2 == 0 else 0)
        gather_ref[face] = (matching & (eighth(row256) == index)).astype(F32).astype(BF16)

    squared = dot(speed_ref[...], widen)
    squared = squared * squared

    def flow_stage(stage):
        for copy in halos[stage]:
            copy.wait_recv()
        fields = flow[stage].reshape(5, 8, 8, 128)
        along_x = jnp.concatenate(
            [halo_recv[stage, 0][:, None], fields, halo_recv[stage, 1][:, None]], 1
        )
        part_x = sweep(along_x, 0)
        along_y = jnp.stack(
            [halo_recv[stage, 2]]
            + [flow[stage, :, pl.ds(y, 8, stride=8), :] for y in range(8)]
            + [halo_recv[stage, 3]],
            1,
        )
        part_y = jnp.stack(sweep(along_y, 1), 0)
        for y in range(8):
            turned[:, pl.ds(y, 8, stride=8), :] = part_y[:, y]
        low, high = (
            jnp.stack(
                [
                    jnp.broadcast_to(halo_recv[stage, side][:, :, x : x + 1], (5, 8, 128))
                    for x in range(8)
                ],
                1,
            )
            for side in (4, 5)
        )
        below = jnp.where(lane == 0, low, pltpu.roll(fields, 1, 3))
        above = jnp.where(lane == 127, high, pltpu.roll(fields, 127, 3))
        part_z = [part[0] for part in sweep(jnp.stack([below, fields, above], 1), 2)]
        part_y = [turned[index].reshape(8, 8, 128) for index in range(7)]
        keep, scale = BLEND[stage]
        for index in range(5):
            rate = part_x[index] + part_y[index] + part_z[index]
            result = scale * (fields[index] + TIME_STEP * rate)
            if stage:
                result = keep * flow[0, index].reshape(8, 8, 128) + result
            if stage < 2:
                flow[stage + 1, index] = result.reshape(64, 128)
            else:
                flow_out[index] = result
        if stage < 2:
            pack_halos(stage + 1)
            halos.append(halo_copies(stage + 1))
            for copy in halos[-1]:
                copy.start()
        inverse = 1.0 / fields[0]
        speed = [fields[1 + part] * inverse for part in range(3)]
        curl = [part_y[6] - part_z[6], part_z[5] - part_x[6], part_x[5] - part_y[5]]
        lamb = [
            (curl[1] * speed[2] - curl[2] * speed[1]).reshape(64, 128),
            (curl[2] * speed[0] - curl[0] * speed[2]).reshape(64, 128),
            (curl[0] * speed[1] - curl[1] * speed[0]).reshape(64, 128),
        ]
        modes = dot(pair_ref[...], jnp.concatenate(lamb, 1))
        empty = jnp.zeros((64, 128), F32)
        doubled = []
        for part in range(3):
            piece = modes[:, 128 * part : 128 * part + 128]
            doubled.append(jnp.concatenate([piece, empty], 1))
            doubled.append(jnp.concatenate([empty, piece], 1))
        routed = dot_nt(route_ref[...], jnp.concatenate(doubled, 0))
        for part in range(3):
            packed[stage, :, part] = routed[:, 128 * part : 128 * part + 128].reshape(n_y, 8, 128)
        spread(*packet_args(stage))

    def own_rate(stage):
        state = sound[stage]
        mixed = dot(slope_ref[...], jnp.concatenate([state[0], state[1], state[2]], 1))
        depth = dot(jnp.concatenate([state[0], state[3]], 0), slope_z_ref[...])
        rate_ref[0] = -squared * (mixed[:64, 128:256] + mixed[64:, 256:] + depth[64:])
        rate_ref[1] = -mixed[:64, :128]
        rate_ref[2] = -mixed[64:, :128]
        rate_ref[3] = -depth[:64]
        for copy in traces[stage]:
            copy.wait_recv()
        jumps = []
        for face in range(6):
            axis, upper = face // 2, face % 2
            if upper:
                sides = [trace[stage, 0, axis], trace_recv[stage, 1, axis]]
            else:
                sides = [trace_recv[stage, 0, axis], trace[stage, 1, axis]]
            found = pick(
                jnp.concatenate([side.reshape(32, 128) for side in sides], 1), gather_ref[face]
            )
            jumps.append(PENALTY * (found.reshape(4, 8, 128) - trace[stage, upper, axis]))
        rate_ref[:, 0:8, :] += jumps[0]
        rate_ref[:, 56:64, :] += jumps[1]
        rate_ref[:, pl.ds(0, 8, stride=8), :] += jumps[2]
        rate_ref[:, pl.ds(7, 8, stride=8), :] += jumps[3]
        for x in range(8):
            low = pltpu.roll(jumps[4], 128 - x, 2) if x else jumps[4]
            high = pltpu.roll(jumps[5], 7 - x, 2) if x < 7 else jumps[5]
            rate_ref[:, 8 * x : 8 * x + 8, :] += jnp.where(
                digit == 0, low, jnp.where(digit == 7, high, 0.0)
            )

    def add_sources(stage):
        spread_whole(*packet_args(stage)).wait_recv()
        pieces = []
        for part in range(3):
            across = arrived[stage, :, part].reshape(rows_out, 128).T
            pieces.append(jnp.concatenate([across[:64], across[64:]], 1))
        source = pick(jnp.concatenate(pieces, 0), place_ref[...])
        keep, scale = BLEND[stage]
        results = []
        for field in range(4):
            rate = rate_ref[field]
            if field:
                rate = rate + source[64 * (field - 1) : 64 * field]
            result = scale * (sound[stage, field] + TIME_STEP * rate)
            if stage:
                result = keep * sound[0, field] + result
            results.append(result)
        return results

    flow_stage(0)

    spread_whole(*label_args()).wait_recv()
    come = labels_recv[...].reshape(rows_out, 128)
    wanted = (eighth(column) + 1).astype(F32)
    for slot in range(2):
        place_ref[slot * rows_out : (slot + 1) * rows_out, :] = (
            (same_digit & (come[:, 64 * slot : 64 * slot + 1] == wanted)).astype(F32).astype(BF16)
        )
    own_rate(0)

    flow_stage(1)
    flow_stage(2)
    for stage in range(3):
        results = add_sources(stage)
        if stage < 2:
            for field in range(4):
                sound[stage + 1, field] = results[field]
            take_traces(stage + 1)
            traces.append(trace_copies(stage + 1))
            for copy in traces[-1]:
                copy.start()
            own_rate(stage + 1)
        else:
            final = swap_groups(jnp.concatenate(results, 0).reshape(16, 16, 128))
            for field in range(4):
                for part in range(4):
                    sound_out[:, field, 128 * part : 128 * part + 128] = final[4 * field + part]

    for stage in range(3):
        for copy in halos[stage] + traces[stage]:
            copy.wait_send()
        spread_whole(*packet_args(stage)).wait_send()
    spread_whole(*label_args()).wait_send()


def solution(mesh):
    sizes = (mesh.shape["fx"], mesh.shape["fy"], mesh.shape["fz"])
    n_y = sizes[1]

    def per_device(
        density,
        velocity,
        pressure,
        acoustic,
        sound_speed,
        derivative,
        mode_basis,
        neighbours,
        block_owner,
        block_element,
    ):
        vmem = pl.BlockSpec(memory_space=pltpu.VMEM)
        return pl.pallas_call(
            functools.partial(kernel, sizes),
            out_shape=(
                jax.ShapeDtypeStruct((5, 8, 8, 128), F32),
                jax.ShapeDtypeStruct((16, 4, 512), F32),
            ),
            in_specs=[vmem] * 10,
            out_specs=(vmem, vmem),
            scratch_shapes=[
                pltpu.VMEM((3, 5, 64, 128), F32),
                pltpu.VMEM((3, 4, 5, 8, 128), F32),
                pltpu.VMEM((3, 6, 5, 8, 128), F32),
                pltpu.VMEM((7, 64, 128), F32),
                pltpu.VMEM((3, 4, 64, 128), F32),
                pltpu.VMEM((3, 2, 3, 4, 8, 128), F32),
                pltpu.VMEM((3, 2, 3, 4, 8, 128), F32),
                pltpu.VMEM((4, 64, 128), F32),
                pltpu.VMEM((3, n_y, 3, 8, 128), F32),
                pltpu.VMEM((3, n_y, 3, 8, 128), F32),
                pltpu.VMEM((n_y, 8, 128), F32),
                pltpu.VMEM((n_y, 8, 128), F32),
                pltpu.VMEM((6, 256, 128), BF16),
                pltpu.VMEM((16 * n_y, 128), BF16),
                pltpu.VMEM((8 * n_y, 256), F32),
                pltpu.VMEM((64, 64), F32),
                pltpu.VMEM((128, 64), F32),
                pltpu.VMEM((128, 128), F32),
                pltpu.SemaphoreType.DMA((3, 6)),
                pltpu.SemaphoreType.DMA((3, 6)),
                pltpu.SemaphoreType.DMA((3, 2)),
                pltpu.SemaphoreType.DMA((3, 2)),
                pltpu.SemaphoreType.DMA((3,)),
                pltpu.SemaphoreType.DMA((3,)),
                pltpu.SemaphoreType.DMA((1,)),
                pltpu.SemaphoreType.DMA((1,)),
            ],
            compiler_params=pltpu.CompilerParams(
                collective_id=0, has_side_effects=True, vmem_limit_bytes=40 * 1024 * 1024
            ),
            name="step",
        )(
            density,
            velocity,
            pressure,
            acoustic,
            sound_speed.reshape(1, 16),
            derivative,
            mode_basis,
            neighbours,
            block_owner.reshape(1, 16),
            block_element.reshape(1, 16),
        )

    placed = (
        P("fx", "fy", "fz"),
        P(None, "fx", "fy", "fz"),
        P("fx", "fy", "fz"),
        P(("fx", "fy", "fz"), None, None),
        P(("fx", "fy", "fz")),
        P(),
        P(),
        P(("fx", "fy", "fz"), None),
        P("fx", "fy", "fz", None, None),
        P("fx", "fy", "fz", None),
    )
    return jax.shard_map(
        per_device,
        mesh=mesh,
        in_specs=placed,
        out_specs=(P(None, "fx", "fy", "fz"), P(("fx", "fy", "fz"), None, None)),
        check_vma=False,
    )
```

```python
import functools

import jax
import jax.numpy as jnp
from jax import lax
from jax.experimental import pallas as pl
from jax.experimental.pallas import tpu as pltpu
from jax.sharding import PartitionSpec as P

HEAT_RATIO = 1.4
TIME_STEP = 0.1
VISCOSITY = 0.05
PENALTY = 0.5
HIGHEST = lax.Precision.HIGHEST
MESH = pl.DeviceIdType.MESH
BLEND = ((0.0, 1.0), (0.75, 0.25), (1.0 / 3.0, 2.0 / 3.0))
F32 = jnp.float32
BF16 = jnp.bfloat16


def dot(a, b):
    return jnp.dot(a, b, precision=HIGHEST, preferred_element_type=F32)


def dot_nt(a, b):
    return lax.dot_general(
        a, b, (((1,), (1,)), ((), ())), precision=HIGHEST, preferred_element_type=F32
    )


def pick(values, chooser):
    rows = values.shape[0]
    high = values.astype(BF16)
    rest = values - high.astype(F32)
    middle = rest.astype(BF16)
    low = (rest - middle.astype(F32)).astype(BF16)
    parts = jnp.dot(
        jnp.concatenate([high, middle, low], 0), chooser, preferred_element_type=F32
    )
    return parts[:rows] + parts[rows : 2 * rows] + parts[2 * rows :]


def iota(shape, dim):
    return lax.broadcasted_iota(jnp.int32, shape, dim)


def eighth(values):
    return lax.shift_right_logical(values, 3)


def repeat_rows(matrix, count, by_block, turned=False):
    rows, columns = iota((count, 8), 0), iota((count, 8), 1)
    chooser = ((eighth(rows) if by_block else rows & 7) == columns).astype(F32)
    if turned:
        return dot_nt(chooser, dot(chooser, matrix))
    return dot_nt(dot(chooser, matrix), chooser)


def swap_groups(values):
    rows, groups = iota((16, 128), 0), eighth(iota((16, 128), 1))
    for bit in range(4):
        step = 1 << bit
        row_bit, group_bit = (rows & step) != 0, (groups & step) != 0
        down = pltpu.roll(pltpu.roll(values, 16 - step, 1), 8 * step, 2)
        up = pltpu.roll(pltpu.roll(values, step, 1), 128 - 8 * step, 2)
        values = jnp.where(
            (row_bit == group_bit)[None], values, jnp.where(group_bit[None], down, up)
        )
    return values


def sweep(cells, along):
    density, momentum, energy = cells[0], cells[1:4], cells[4]
    inverse = 1.0 / density
    velocity = [part * inverse for part in momentum]
    kinetic = sum(part * speed for part, speed in zip(momentum, velocity))
    pressure = (HEAT_RATIO - 1.0) * (energy - 0.5 * kinetic)
    normal = velocity[along]
    signal = jnp.abs(normal) + jnp.sqrt(HEAT_RATIO * jnp.abs(pressure) * inverse)
    half_speed = 0.5 * jnp.maximum(signal[:-1], signal[1:])
    fluxes = [momentum[along]] + [part * normal for part in momentum] + [(energy + pressure) * normal]
    fluxes[1 + along] = fluxes[1 + along] + pressure
    rates = []
    for index, (flux, cell) in enumerate(zip(fluxes, cells)):
        gap = cell[1:] - cell[:-1]
        face = 0.5 * (flux[:-1] + flux[1:]) - half_speed * gap
        rate = face[:-1] - face[1:]
        if 1 <= index <= 3:
            rate = rate + VISCOSITY * (gap[1:] - gap[:-1])
        rates.append(rate)
    slopes = [0.5 * (velocity[c][2:] - velocity[c][:-2]) for c in range(3) if c != along]
    return rates + slopes


def kernel(
    sizes,
    density_in,
    velocity_in,
    pressure_in,
    acoustic_in,
    speed_in,
    derivative_in,
    basis_in,
    neighbour_in,
    owner_in,
    element_in,
    flow_out,
    sound_out,
    flow,
    halo_send,
    halo_recv,
    turned,
    sound,
    trace,
    trace_recv,
    rate_ref,
    packed,
    arrived,
    labels,
    labels_recv,
    gather_ref,
    place_ref,
    route_ref,
    pair_ref,
    slope_ref,
    slope_z_ref,
    halo_out_sem,
    halo_in_sem,
    trace_out_sem,
    trace_in_sem,
    packed_out_sem,
    packed_in_sem,
    label_out_sem,
    label_in_sem,
    density_ref,
    velocity_ref,
    pressure_ref,
    acoustic_ref,
    speed_ref,
    derivative_ref,
    basis_ref,
    neighbour_ref,
    owner_ref,
    element_ref,
    load_sem,
):
    n_x, n_y, n_z = sizes
    fx, fy, fz = lax.axis_index("fx"), lax.axis_index("fy"), lax.axis_index("fz")
    place = (fx * n_y + fy) * n_z + fz
    total = n_x * n_y * n_z

    def device_at(index):
        return (index // (n_y * n_z), (index // n_z) % n_y, index % n_z)

    after, before = device_at((place + 1) % total), device_at((place + total - 1) % total)
    beside = [
        ((fx + 1) % n_x, fy, fz),
        ((fx + n_x - 1) % n_x, fy, fz),
        (fx, (fy + 1) % n_y, fz),
        (fx, (fy + n_y - 1) % n_y, fz),
        (fx, fy, (fz + 1) % n_z),
        (fx, fy, (fz + n_z - 1) % n_z),
    ]
    barrier = pltpu.get_barrier_semaphore()
    for device in [beside[0], beside[1], beside[4], beside[5], after, before]:
        pl.semaphore_signal(barrier, inc=1, device_id=device, device_id_type=MESH)

    @pl.loop(1, n_y)
    def _(step):
        pl.semaphore_signal(
            barrier, inc=1, device_id=(fx, (fy + step) % n_y, fz), device_id_type=MESH
        )

    loads = [
        pltpu.make_async_copy(source, target, load_sem.at[index])
        for index, (source, target) in enumerate(
            (
                (velocity_in, velocity_ref),
                (density_in, density_ref),
                (pressure_in, pressure_ref),
                (acoustic_in, acoustic_ref),
                (owner_in, owner_ref),
                (element_in, element_ref),
                (basis_in, basis_ref),
                (derivative_in, derivative_ref),
                (neighbour_in, neighbour_ref),
                (speed_in, speed_ref),
            )
        )
    ]
    for copy in loads:
        copy.start()

    lane = iota((8, 128), 1)
    digit = lane & 7

    def pack_halos(stage):
        for side, row in ((0, 7), (1, 0)):
            halo_send[stage, side] = flow[stage, :, pl.ds(row, 8, stride=8), :]
        ends = [jnp.zeros((5, 8, 128), F32)] * 2
        for x in range(8):
            plane = flow[stage, :, 8 * x : 8 * x + 8, :]
            ends[0] = jnp.where(lane == x, pltpu.roll(plane, x + 1, 2), ends[0])
            ends[1] = jnp.where(lane == x, pltpu.roll(plane, x, 2) if x else plane, ends[1])
        halo_send[stage, 2], halo_send[stage, 3] = ends

    def halo_copies(stage):
        sources = [flow.at[stage, :, pl.ds(56, 8), :], flow.at[stage, :, pl.ds(0, 8), :]]
        sources += [halo_send.at[stage, index] for index in range(4)]
        return [
            pltpu.make_async_remote_copy(
                src_ref=source,
                dst_ref=halo_recv.at[stage, index],
                send_sem=halo_out_sem.at[stage, index],
                recv_sem=halo_in_sem.at[stage, index],
                device_id=beside[index],
                device_id_type=MESH,
            )
            for index, source in enumerate(sources)
        ]

    def take_traces(stage):
        trace[stage, 0, 0] = sound[stage, :, 0:8, :]
        trace[stage, 1, 0] = sound[stage, :, 56:64, :]
        trace[stage, 0, 1] = sound[stage, :, pl.ds(0, 8, stride=8), :]
        trace[stage, 1, 1] = sound[stage, :, pl.ds(7, 8, stride=8), :]
        ends = [jnp.zeros((4, 8, 128), F32)] * 2
        for x in range(8):
            plane = sound[stage, :, 8 * x : 8 * x + 8, :]
            ends[0] = jnp.where(digit == x, pltpu.roll(plane, x, 2) if x else plane, ends[0])
            ends[1] = jnp.where(digit == x, pltpu.roll(plane, 121 + x, 2) if x < 7 else plane, ends[1])
        trace[stage, 0, 2], trace[stage, 1, 2] = ends

    def trace_copies(stage):
        return [
            pltpu.make_async_remote_copy(
                src_ref=trace.at[stage, 1 - side],
                dst_ref=trace_recv.at[stage, side],
                send_sem=trace_out_sem.at[stage, side],
                recv_sem=trace_in_sem.at[stage, side],
                device_id=device,
                device_id_type=MESH,
            )
            for side, device in ((0, after), (1, before))
        ]

    def spread(args, first=0, last=n_y):
        source, target, out_sem, in_sem = args

        @pl.loop(first, last)
        def _(peer):
            @pl.when(peer != fy)
            def _():
                pltpu.make_async_remote_copy(
                    src_ref=source.at[peer],
                    dst_ref=target.at[fy],
                    send_sem=out_sem,
                    recv_sem=in_sem,
                    device_id=(fx, peer, fz),
                    device_id_type=MESH,
                ).start()

    def keep_own(args):
        source, target = args[:2]
        target[fy] = source[fy]

    def spread_whole(source, target, out_sem, in_sem):
        return pltpu.make_async_remote_copy(
            src_ref=source.at[pl.ds(0, n_y - 1)],
            dst_ref=target.at[pl.ds(0, n_y - 1)],
            send_sem=out_sem,
            recv_sem=in_sem,
            device_id=beside[2],
            device_id_type=MESH,
        )

    def label_args():
        return (labels, labels_recv, label_out_sem.at[0], label_in_sem.at[0])

    def packet_args(stage):
        return (
            packed.at[stage],
            arrived.at[stage],
            packed_out_sem.at[stage],
            packed_in_sem.at[stage],
        )

    for copy in loads[:3]:
        copy.wait()
    density = density_ref[...].reshape(64, 128)
    speeds = velocity_ref[...].reshape(3, 64, 128)
    energy = pressure_ref[...].reshape(64, 128) / (HEAT_RATIO - 1.0) + 0.5 * density * (
        speeds[0] * speeds[0] + speeds[1] * speeds[1] + speeds[2] * speeds[2]
    )
    flow[0, 0] = density
    for part in range(3):
        flow[0, 1 + part] = density * speeds[part]
    flow[0, 4] = energy
    pack_halos(0)

    pl.semaphore_wait(barrier, 6 + n_y - 1)
    halos = [halo_copies(0)]
    for copy in halos[0]:
        copy.start()

    for copy in loads[3:]:
        copy.wait()
    nodes = jnp.stack(
        [
            acoustic_ref[:, field, 128 * part : 128 * part + 128]
            for field in range(4)
            for part in range(4)
        ],
        0,
    )
    sound[0] = swap_groups(nodes).reshape(4, 64, 128)
    take_traces(0)
    traces = [trace_copies(0)]
    for copy in traces[0]:
        copy.start()

    widen = (iota((16, 128), 0) == eighth(iota((16, 128), 1))).astype(F32)
    owner = dot(owner_ref[...].astype(F32), widen)
    element = dot(element_ref[...].astype(F32), widen)
    rows_out = 8 * n_y
    row, column = iota((rows_out, 128), 0), iota((rows_out, 128), 1)
    same_digit = (row & 7) == (column & 7)
    earlier = (
        (eighth(iota((128, 128), 0)) < eighth(iota((128, 128), 1)))
        & ((iota((128, 128), 0) & 7) == 0)
    ).astype(F32)
    named = owner.astype(jnp.int32) == eighth(row)
    count = jnp.dot(named.astype(BF16), earlier.astype(BF16), preferred_element_type=F32)
    first, second = named & (count < 0.5), named & (count > 0.5)
    mark = jnp.where((column & 7) == 0, element + 1.0, 0.0)
    label = jnp.where(
        column < 64,
        jnp.sum(jnp.where(first, mark, 0.0), 1, keepdims=True),
        jnp.sum(jnp.where(second, mark, 0.0), 1, keepdims=True),
    )
    labels[...] = label.reshape(n_y, 8, 128)
    spread(label_args())
    keep_own(label_args())

    basis = basis_ref[...]
    tiled = repeat_rows(basis, 128, False)[:rows_out]
    route_ref[:, 0:128] = jnp.where(first, tiled, 0.0)
    route_ref[:, 128:256] = jnp.where(second, tiled, 0.0)
    pair_ref[...] = repeat_rows(basis, 64, True) * repeat_rows(basis, 64, False)

    derivative = derivative_ref[...]
    row64, column64 = iota((64, 64), 0), iota((64, 64), 1)
    slope_ref[0:64, :] = jnp.where(
        (row64 & 7) == (column64 & 7), repeat_rows(derivative, 64, True), 0.0
    )
    slope_ref[64:128, :] = jnp.where(
        eighth(row64) == eighth(column64), repeat_rows(derivative, 64, False), 0.0
    )
    row128, column128 = iota((128, 128), 0), iota((128, 128), 1)
    slope_z_ref[...] = jnp.where(
        eighth(row128) == eighth(column128), repeat_rows(derivative, 128, False, True), 0.0
    )

    local = (neighbour_ref[...] - place * 16).astype(F32)
    nearby = dot(local, widen).astype(jnp.int32)
    row256, column256 = iota((256, 128), 0), iota((256, 128), 1)
    matching = (row256 & 7) == (column256 & 7)
    for face in range(6):
        index = nearby[face : face + 1] + (16 if face % 2 == 0 else 0)
        gather_ref[face] = (matching & (eighth(row256) == index)).astype(F32).astype(BF16)

    squared = dot(speed_ref[...], widen)
    squared = squared * squared

    def flow_stage(stage):
        for copy in halos[stage]:
            copy.wait_recv()
        fields = flow[stage].reshape(5, 8, 8, 128)
        along_x = jnp.concatenate(
            [halo_recv[stage, 0][:, None], fields, halo_recv[stage, 1][:, None]], 1
        )
        part_x = sweep(along_x, 0)
        along_y = jnp.stack(
            [halo_recv[stage, 2]]
            + [flow[stage, :, pl.ds(y, 8, stride=8), :] for y in range(8)]
            + [halo_recv[stage, 3]],
            1,
        )
        part_y = jnp.stack(sweep(along_y, 1), 0)
        for y in range(8):
            turned[:, pl.ds(y, 8, stride=8), :] = part_y[:, y]
        low, high = (
            jnp.stack(
                [
                    jnp.broadcast_to(halo_recv[stage, side][:, :, x : x + 1], (5, 8, 128))
                    for x in range(8)
                ],
                1,
            )
            for side in (4, 5)
        )
        below = jnp.where(lane == 0, low, pltpu.roll(fields, 1, 3))
        above = jnp.where(lane == 127, high, pltpu.roll(fields, 127, 3))
        part_z = [part[0] for part in sweep(jnp.stack([below, fields, above], 1), 2)]
        part_y = [turned[index].reshape(8, 8, 128) for index in range(7)]
        keep, scale = BLEND[stage]
        for index in range(5):
            rate = part_x[index] + part_y[index] + part_z[index]
            result = scale * (fields[index] + TIME_STEP * rate)
            if stage:
                result = keep * flow[0, index].reshape(8, 8, 128) + result
            if stage < 2:
                flow[stage + 1, index] = result.reshape(64, 128)
            else:
                flow_out[index] = result
        if stage < 2:
            pack_halos(stage + 1)
            halos.append(halo_copies(stage + 1))
            for copy in halos[-1]:
                copy.start()
        inverse = 1.0 / fields[0]
        speed = [fields[1 + part] * inverse for part in range(3)]
        curl = [part_y[6] - part_z[6], part_z[5] - part_x[6], part_x[5] - part_y[5]]
        lamb = [
            (curl[1] * speed[2] - curl[2] * speed[1]).reshape(64, 128),
            (curl[2] * speed[0] - curl[0] * speed[2]).reshape(64, 128),
            (curl[0] * speed[1] - curl[1] * speed[0]).reshape(64, 128),
        ]
        modes = dot(pair_ref[...], jnp.concatenate(lamb, 1))
        empty = jnp.zeros((64, 128), F32)
        doubled = []
        for part in range(3):
            piece = modes[:, 128 * part : 128 * part + 128]
            doubled.append(jnp.concatenate([piece, empty], 1))
            doubled.append(jnp.concatenate([empty, piece], 1))
        routed = dot_nt(route_ref[...], jnp.concatenate(doubled, 0))
        for part in range(3):
            packed[stage, :, part] = routed[:, 128 * part : 128 * part + 128].reshape(n_y, 8, 128)

    def own_rate(stage):
        state = sound[stage]
        mixed = dot(slope_ref[...], jnp.concatenate([state[0], state[1], state[2]], 1))
        depth = dot(jnp.concatenate([state[0], state[3]], 0), slope_z_ref[...])
        rate_ref[0] = -squared * (mixed[:64, 128:256] + mixed[64:, 256:] + depth[64:])
        rate_ref[1] = -mixed[:64, :128]
        rate_ref[2] = -mixed[64:, :128]
        rate_ref[3] = -depth[:64]
        for copy in traces[stage]:
            copy.wait_recv()
        jumps = []
        for face in range(6):
            axis, upper = face // 2, face % 2
            if upper:
                sides = [trace[stage, 0, axis], trace_recv[stage, 1, axis]]
            else:
                sides = [trace_recv[stage, 0, axis], trace[stage, 1, axis]]
            found = pick(
                jnp.concatenate([side.reshape(32, 128) for side in sides], 1), gather_ref[face]
            )
            jumps.append(PENALTY * (found.reshape(4, 8, 128) - trace[stage, upper, axis]))
        rate_ref[:, 0:8, :] += jumps[0]
        rate_ref[:, 56:64, :] += jumps[1]
        rate_ref[:, pl.ds(0, 8, stride=8), :] += jumps[2]
        rate_ref[:, pl.ds(7, 8, stride=8), :] += jumps[3]
        for x in range(8):
            low = pltpu.roll(jumps[4], 128 - x, 2) if x else jumps[4]
            high = pltpu.roll(jumps[5], 7 - x, 2) if x < 7 else jumps[5]
            rate_ref[:, 8 * x : 8 * x + 8, :] += jnp.where(
                digit == 0, low, jnp.where(digit == 7, high, 0.0)
            )

    def add_sources(stage):
        spread_whole(*packet_args(stage)).wait_recv()
        pieces = []
        for part in range(3):
            across = arrived[stage, :, part].reshape(rows_out, 128).T
            pieces.append(jnp.concatenate([across[:64], across[64:]], 1))
        source = pick(jnp.concatenate(pieces, 0), place_ref[...])
        keep, scale = BLEND[stage]
        results = []
        for field in range(4):
            rate = rate_ref[field]
            if field:
                rate = rate + source[64 * (field - 1) : 64 * field]
            result = scale * (sound[stage, field] + TIME_STEP * rate)
            if stage:
                result = keep * sound[0, field] + result
            results.append(result)
        return results

    flow_stage(0)
    spread(packet_args(0))
    keep_own(packet_args(0))

    spread_whole(*label_args()).wait_recv()
    come = labels_recv[...].reshape(rows_out, 128)
    wanted = (eighth(column) + 1).astype(F32)
    for slot in range(2):
        place_ref[slot * rows_out : (slot + 1) * rows_out, :] = (
            (same_digit & (come[:, 64 * slot : 64 * slot + 1] == wanted)).astype(F32).astype(BF16)
        )
    own_rate(0)

    flow_stage(1)
    spread(packet_args(1))
    keep_own(packet_args(1))
    flow_stage(2)
    spread(packet_args(2), 0, 5)
    keep_own(packet_args(2))
    for stage in range(2):
        for field, result in enumerate(add_sources(stage)):
            sound[stage + 1, field] = result
        take_traces(stage + 1)
        traces.append(trace_copies(stage + 1))
        for copy in traces[-1]:
            copy.start()
        if stage == 0:
            spread(packet_args(2), 5)
        own_rate(stage + 1)
    final = swap_groups(jnp.concatenate(add_sources(2), 0).reshape(16, 16, 128))
    for field in range(4):
        for part in range(4):
            sound_out[:, field, 128 * part : 128 * part + 128] = final[4 * field + part]

    for stage in range(3):
        for copy in halos[stage] + traces[stage]:
            copy.wait_send()
        spread_whole(*packet_args(stage)).wait_send()
    spread_whole(*label_args()).wait_send()


def solution(mesh):
    sizes = (mesh.shape["fx"], mesh.shape["fy"], mesh.shape["fz"])
    n_y = sizes[1]

    def per_device(
        density,
        velocity,
        pressure,
        acoustic,
        sound_speed,
        derivative,
        mode_basis,
        neighbours,
        block_owner,
        block_element,
    ):
        vmem, hbm = pl.BlockSpec(memory_space=pltpu.VMEM), pl.BlockSpec(memory_space=pltpu.HBM)
        results = (
            jax.ShapeDtypeStruct((5, 8, 8, 128), F32),
            jax.ShapeDtypeStruct((16, 4, 512), F32),
        )
        return pl.pallas_call(
            functools.partial(kernel, sizes),
            out_shape=results,
            in_specs=[hbm] * 10,
            out_specs=(vmem, vmem),
            scratch_shapes=[
                pltpu.VMEM((3, 5, 64, 128), F32),
                pltpu.VMEM((3, 4, 5, 8, 128), F32),
                pltpu.VMEM((3, 6, 5, 8, 128), F32),
                pltpu.VMEM((7, 64, 128), F32),
                pltpu.VMEM((3, 4, 64, 128), F32),
                pltpu.VMEM((3, 2, 3, 4, 8, 128), F32),
                pltpu.VMEM((3, 2, 3, 4, 8, 128), F32),
                pltpu.VMEM((4, 64, 128), F32),
                pltpu.VMEM((3, n_y, 3, 8, 128), F32),
                pltpu.VMEM((3, n_y, 3, 8, 128), F32),
                pltpu.VMEM((n_y, 8, 128), F32),
                pltpu.VMEM((n_y, 8, 128), F32),
                pltpu.VMEM((6, 256, 128), BF16),
                pltpu.VMEM((16 * n_y, 128), BF16),
                pltpu.VMEM((8 * n_y, 256), F32),
                pltpu.VMEM((64, 64), F32),
                pltpu.VMEM((128, 64), F32),
                pltpu.VMEM((128, 128), F32),
                pltpu.SemaphoreType.DMA((3, 6)),
                pltpu.SemaphoreType.DMA((3, 6)),
                pltpu.SemaphoreType.DMA((3, 2)),
                pltpu.SemaphoreType.DMA((3, 2)),
                pltpu.SemaphoreType.DMA((3,)),
                pltpu.SemaphoreType.DMA((3,)),
                pltpu.SemaphoreType.DMA((1,)),
                pltpu.SemaphoreType.DMA((1,)),
                pltpu.VMEM((8, 8, 128), F32),
                pltpu.VMEM((3, 8, 8, 128), F32),
                pltpu.VMEM((8, 8, 128), F32),
                pltpu.VMEM((16, 4, 512), F32),
                pltpu.VMEM((1, 16), F32),
                pltpu.VMEM((8, 8), F32),
                pltpu.VMEM((8, 8), F32),
                pltpu.VMEM((6, 16), jnp.int32),
                pltpu.VMEM((1, 16), jnp.int32),
                pltpu.VMEM((1, 16), jnp.int32),
                pltpu.SemaphoreType.DMA((10,)),
            ],
            compiler_params=pltpu.CompilerParams(
                collective_id=0, has_side_effects=True, vmem_limit_bytes=40 * 1024 * 1024
            ),
            name="step",
        )(
            *(
                pltpu.with_memory_space_constraint(value, pltpu.HBM)
                for value in (
                    density,
                    velocity,
                    pressure,
                    acoustic,
                    sound_speed.reshape(1, 16),
                    derivative,
                    mode_basis,
                    neighbours.T,
                    block_owner.reshape(1, 16),
                    block_element.reshape(1, 16),
                )
            )
        )

    placed = (
        P("fx", "fy", "fz"),
        P(None, "fx", "fy", "fz"),
        P("fx", "fy", "fz"),
        P(("fx", "fy", "fz"), None, None),
        P(("fx", "fy", "fz")),
        P(),
        P(),
        P(("fx", "fy", "fz"), None),
        P("fx", "fy", "fz", None, None),
        P("fx", "fy", "fz", None),
    )
    return jax.shard_map(
        per_device,
        mesh=mesh,
        in_specs=placed,
        out_specs=(P(None, "fx", "fy", "fz"), P(("fx", "fy", "fz"), None, None)),
        check_vma=False,
    )
```

```python
import functools

import jax
import jax.numpy as jnp
from jax import lax
from jax.experimental import pallas as pl
from jax.experimental.pallas import tpu as pltpu
from jax.sharding import PartitionSpec as P

HEAT_RATIO = 1.4
TIME_STEP = 0.1
VISCOSITY = 0.05
PENALTY = 0.5
HIGHEST = lax.Precision.HIGHEST
MESH = pl.DeviceIdType.MESH
BLEND = ((0.0, 1.0), (0.75, 0.25), (1.0 / 3.0, 2.0 / 3.0))
F32 = jnp.float32
BF16 = jnp.bfloat16


def dot(a, b):
    return jnp.dot(a, b, precision=HIGHEST, preferred_element_type=F32)


def dot_nt(a, b):
    return lax.dot_general(
        a, b, (((1,), (1,)), ((), ())), precision=HIGHEST, preferred_element_type=F32
    )


def pick(values, chooser):
    rows = values.shape[0]
    high = values.astype(BF16)
    rest = values - high.astype(F32)
    middle = rest.astype(BF16)
    low = (rest - middle.astype(F32)).astype(BF16)
    parts = jnp.dot(
        jnp.concatenate([high, middle, low], 0), chooser, preferred_element_type=F32
    )
    return parts[:rows] + parts[rows : 2 * rows] + parts[2 * rows :]


def iota(shape, dim):
    return lax.broadcasted_iota(jnp.int32, shape, dim)


def eighth(values):
    return lax.shift_right_logical(values, 3)


def repeat_rows(matrix, count, by_block, turned=False):
    rows, columns = iota((count, 8), 0), iota((count, 8), 1)
    chooser = ((eighth(rows) if by_block else rows & 7) == columns).astype(F32)
    if turned:
        return dot_nt(chooser, dot(chooser, matrix))
    return dot_nt(dot(chooser, matrix), chooser)


def swap_groups(values):
    rows, groups = iota((16, 128), 0), eighth(iota((16, 128), 1))
    for bit in range(4):
        step = 1 << bit
        row_bit, group_bit = (rows & step) != 0, (groups & step) != 0
        down = pltpu.roll(pltpu.roll(values, 16 - step, 1), 8 * step, 2)
        up = pltpu.roll(pltpu.roll(values, step, 1), 128 - 8 * step, 2)
        values = jnp.where(
            (row_bit == group_bit)[None], values, jnp.where(group_bit[None], down, up)
        )
    return values


def sweep(cells, along):
    density, momentum, energy = cells[0], cells[1:4], cells[4]
    inverse = 1.0 / density
    velocity = [part * inverse for part in momentum]
    kinetic = sum(part * speed for part, speed in zip(momentum, velocity))
    pressure = (HEAT_RATIO - 1.0) * (energy - 0.5 * kinetic)
    normal = velocity[along]
    signal = jnp.abs(normal) + jnp.sqrt(HEAT_RATIO * jnp.abs(pressure) * inverse)
    half_speed = 0.5 * jnp.maximum(signal[:-1], signal[1:])
    fluxes = [momentum[along]] + [part * normal for part in momentum] + [(energy + pressure) * normal]
    fluxes[1 + along] = fluxes[1 + along] + pressure
    rates = []
    for index, (flux, cell) in enumerate(zip(fluxes, cells)):
        gap = cell[1:] - cell[:-1]
        face = 0.5 * (flux[:-1] + flux[1:]) - half_speed * gap
        rate = face[:-1] - face[1:]
        if 1 <= index <= 3:
            rate = rate + VISCOSITY * (gap[1:] - gap[:-1])
        rates.append(rate)
    slopes = [0.5 * (velocity[c][2:] - velocity[c][:-2]) for c in range(3) if c != along]
    return rates + slopes


def kernel(
    sizes,
    density_in,
    velocity_in,
    pressure_in,
    acoustic_in,
    speed_in,
    derivative_in,
    basis_in,
    neighbour_in,
    owner_in,
    element_in,
    flow_out,
    sound_out,
    flow,
    halo_send,
    halo_recv,
    turned,
    sound,
    trace,
    trace_recv,
    rate_ref,
    packed,
    arrived,
    labels,
    labels_recv,
    gather_ref,
    place_ref,
    route_ref,
    pair_ref,
    slope_ref,
    slope_z_ref,
    halo_out_sem,
    halo_in_sem,
    trace_out_sem,
    trace_in_sem,
    packed_out_sem,
    packed_in_sem,
    label_out_sem,
    label_in_sem,
    density_ref,
    velocity_ref,
    pressure_ref,
    acoustic_ref,
    speed_ref,
    derivative_ref,
    basis_ref,
    neighbour_ref,
    owner_ref,
    element_ref,
    load_sem,
):
    n_x, n_y, n_z = sizes
    fx, fy, fz = lax.axis_index("fx"), lax.axis_index("fy"), lax.axis_index("fz")
    place = (fx * n_y + fy) * n_z + fz
    total = n_x * n_y * n_z

    def device_at(index):
        return (index // (n_y * n_z), (index // n_z) % n_y, index % n_z)

    after, before = device_at((place + 1) % total), device_at((place + total - 1) % total)
    beside = [
        ((fx + 1) % n_x, fy, fz),
        ((fx + n_x - 1) % n_x, fy, fz),
        (fx, (fy + 1) % n_y, fz),
        (fx, (fy + n_y - 1) % n_y, fz),
        (fx, fy, (fz + 1) % n_z),
        (fx, fy, (fz + n_z - 1) % n_z),
    ]
    barrier = pltpu.get_barrier_semaphore()
    for device in [beside[0], beside[1], beside[4], beside[5], after, before]:
        pl.semaphore_signal(barrier, inc=1, device_id=device, device_id_type=MESH)

    @pl.loop(1, n_y)
    def _(step):
        pl.semaphore_signal(
            barrier, inc=1, device_id=(fx, (fy + step) % n_y, fz), device_id_type=MESH
        )

    loads = [
        pltpu.make_async_copy(source, target, load_sem.at[index])
        for index, (source, target) in enumerate(
            (
                (velocity_in, velocity_ref),
                (density_in, density_ref),
                (pressure_in, pressure_ref),
                (acoustic_in, acoustic_ref),
                (owner_in, owner_ref),
                (element_in, element_ref),
                (basis_in, basis_ref),
                (derivative_in, derivative_ref),
                (neighbour_in, neighbour_ref),
                (speed_in, speed_ref),
            )
        )
    ]
    for copy in loads:
        copy.start()

    lane = iota((8, 128), 1)
    digit = lane & 7

    def pack_halos(stage):
        for side, row in ((0, 7), (1, 0)):
            halo_send[stage, side] = flow[stage, :, pl.ds(row, 8, stride=8), :]
        ends = [jnp.zeros((5, 8, 128), F32)] * 2
        for x in range(8):
            plane = flow[stage, :, 8 * x : 8 * x + 8, :]
            ends[0] = jnp.where(lane == x, pltpu.roll(plane, x + 1, 2), ends[0])
            ends[1] = jnp.where(lane == x, pltpu.roll(plane, x, 2) if x else plane, ends[1])
        halo_send[stage, 2], halo_send[stage, 3] = ends

    def halo_copies(stage):
        sources = [flow.at[stage, :, pl.ds(56, 8), :], flow.at[stage, :, pl.ds(0, 8), :]]
        sources += [halo_send.at[stage, index] for index in range(4)]
        return [
            pltpu.make_async_remote_copy(
                src_ref=source,
                dst_ref=halo_recv.at[stage, index],
                send_sem=halo_out_sem.at[stage, index],
                recv_sem=halo_in_sem.at[stage, index],
                device_id=beside[index],
                device_id_type=MESH,
            )
            for index, source in enumerate(sources)
        ]

    def take_traces(stage):
        trace[stage, 0, 0] = sound[stage, :, 0:8, :]
        trace[stage, 1, 0] = sound[stage, :, 56:64, :]
        trace[stage, 0, 1] = sound[stage, :, pl.ds(0, 8, stride=8), :]
        trace[stage, 1, 1] = sound[stage, :, pl.ds(7, 8, stride=8), :]
        ends = [jnp.zeros((4, 8, 128), F32)] * 2
        for x in range(8):
            plane = sound[stage, :, 8 * x : 8 * x + 8, :]
            ends[0] = jnp.where(digit == x, pltpu.roll(plane, x, 2) if x else plane, ends[0])
            ends[1] = jnp.where(digit == x, pltpu.roll(plane, 121 + x, 2) if x < 7 else plane, ends[1])
        trace[stage, 0, 2], trace[stage, 1, 2] = ends

    def trace_copies(stage):
        return [
            pltpu.make_async_remote_copy(
                src_ref=trace.at[stage, 1 - side],
                dst_ref=trace_recv.at[stage, side],
                send_sem=trace_out_sem.at[stage, side],
                recv_sem=trace_in_sem.at[stage, side],
                device_id=device,
                device_id_type=MESH,
            )
            for side, device in ((0, after), (1, before))
        ]

    def spread(args, first=0, last=n_y):
        source, target, out_sem, in_sem = args

        @pl.loop(first, last)
        def _(rank):
            peer = (rank + n_y - 1) % n_y

            @pl.when(peer != fy)
            def _():
                pltpu.make_async_remote_copy(
                    src_ref=source.at[peer],
                    dst_ref=target.at[fy],
                    send_sem=out_sem,
                    recv_sem=in_sem,
                    device_id=(fx, peer, fz),
                    device_id_type=MESH,
                ).start()

    def keep_own(args):
        source, target = args[:2]
        target[fy] = source[fy]

    def spread_whole(source, target, out_sem, in_sem):
        return pltpu.make_async_remote_copy(
            src_ref=source.at[pl.ds(0, n_y - 1)],
            dst_ref=target.at[pl.ds(0, n_y - 1)],
            send_sem=out_sem,
            recv_sem=in_sem,
            device_id=beside[2],
            device_id_type=MESH,
        )

    def label_args():
        return (labels, labels_recv, label_out_sem.at[0], label_in_sem.at[0])

    def packet_args(stage):
        return (
            packed.at[stage],
            arrived.at[stage],
            packed_out_sem.at[stage],
            packed_in_sem.at[stage],
        )

    for copy in loads[:3]:
        copy.wait()
    density = density_ref[...].reshape(64, 128)
    speeds = velocity_ref[...].reshape(3, 64, 128)
    energy = pressure_ref[...].reshape(64, 128) / (HEAT_RATIO - 1.0) + 0.5 * density * (
        speeds[0] * speeds[0] + speeds[1] * speeds[1] + speeds[2] * speeds[2]
    )
    flow[0, 0] = density
    for part in range(3):
        flow[0, 1 + part] = density * speeds[part]
    flow[0, 4] = energy
    pack_halos(0)

    pl.semaphore_wait(barrier, 6 + n_y - 1)
    halos = [halo_copies(0)]
    for copy in halos[0]:
        copy.start()

    for copy in loads[3:]:
        copy.wait()
    nodes = jnp.stack(
        [
            acoustic_ref[:, field, 128 * part : 128 * part + 128]
            for field in range(4)
            for part in range(4)
        ],
        0,
    )
    sound[0] = swap_groups(nodes).reshape(4, 64, 128)
    take_traces(0)
    traces = [trace_copies(0)]
    for copy in traces[0]:
        copy.start()

    widen = (iota((16, 128), 0) == eighth(iota((16, 128), 1))).astype(F32)
    owner = dot(owner_ref[...].astype(F32), widen)
    element = dot(element_ref[...].astype(F32), widen)
    rows_out = 8 * n_y
    row, column = iota((rows_out, 128), 0), iota((rows_out, 128), 1)
    same_digit = (row & 7) == (column & 7)
    earlier = (
        (eighth(iota((128, 128), 0)) < eighth(iota((128, 128), 1)))
        & ((iota((128, 128), 0) & 7) == 0)
    ).astype(F32)
    named = owner.astype(jnp.int32) == eighth(row)
    count = jnp.dot(named.astype(BF16), earlier.astype(BF16), preferred_element_type=F32)
    first, second = named & (count < 0.5), named & (count > 0.5)
    mark = jnp.where((column & 7) == 0, element + 1.0, 0.0)
    label = jnp.where(
        column < 64,
        jnp.sum(jnp.where(first, mark, 0.0), 1, keepdims=True),
        jnp.sum(jnp.where(second, mark, 0.0), 1, keepdims=True),
    )
    labels[...] = label.reshape(n_y, 8, 128)
    spread(label_args())
    keep_own(label_args())

    basis = basis_ref[...]
    tiled = repeat_rows(basis, 128, False)[:rows_out]
    route_ref[:, 0:128] = jnp.where(first, tiled, 0.0)
    route_ref[:, 128:256] = jnp.where(second, tiled, 0.0)
    pair_ref[...] = repeat_rows(basis, 64, True) * repeat_rows(basis, 64, False)

    derivative = derivative_ref[...]
    row64, column64 = iota((64, 64), 0), iota((64, 64), 1)
    slope_ref[0:64, :] = jnp.where(
        (row64 & 7) == (column64 & 7), repeat_rows(derivative, 64, True), 0.0
    )
    slope_ref[64:128, :] = jnp.where(
        eighth(row64) == eighth(column64), repeat_rows(derivative, 64, False), 0.0
    )
    row128, column128 = iota((128, 128), 0), iota((128, 128), 1)
    slope_z_ref[...] = jnp.where(
        eighth(row128) == eighth(column128), repeat_rows(derivative, 128, False, True), 0.0
    )

    local = (neighbour_ref[...] - place * 16).astype(F32)
    nearby = dot(local, widen).astype(jnp.int32)
    row256, column256 = iota((256, 128), 0), iota((256, 128), 1)
    matching = (row256 & 7) == (column256 & 7)
    for face in range(6):
        index = nearby[face : face + 1] + (16 if face % 2 == 0 else 0)
        gather_ref[face] = (matching & (eighth(row256) == index)).astype(F32).astype(BF16)

    squared = dot(speed_ref[...], widen)
    squared = squared * squared

    def flow_stage(stage):
        for copy in halos[stage]:
            copy.wait_recv()
        fields = flow[stage].reshape(5, 8, 8, 128)
        along_x = jnp.concatenate(
            [halo_recv[stage, 0][:, None], fields, halo_recv[stage, 1][:, None]], 1
        )
        part_x = sweep(along_x, 0)
        along_y = jnp.stack(
            [halo_recv[stage, 2]]
            + [flow[stage, :, pl.ds(y, 8, stride=8), :] for y in range(8)]
            + [halo_recv[stage, 3]],
            1,
        )
        part_y = jnp.stack(sweep(along_y, 1), 0)
        for y in range(8):
            turned[:, pl.ds(y, 8, stride=8), :] = part_y[:, y]
        low, high = (
            jnp.stack(
                [
                    jnp.broadcast_to(halo_recv[stage, side][:, :, x : x + 1], (5, 8, 128))
                    for x in range(8)
                ],
                1,
            )
            for side in (4, 5)
        )
        below = jnp.where(lane == 0, low, pltpu.roll(fields, 1, 3))
        above = jnp.where(lane == 127, high, pltpu.roll(fields, 127, 3))
        part_z = [part[0] for part in sweep(jnp.stack([below, fields, above], 1), 2)]
        part_y = [turned[index].reshape(8, 8, 128) for index in range(7)]
        keep, scale = BLEND[stage]
        for index in range(5):
            rate = part_x[index] + part_y[index] + part_z[index]
            result = scale * (fields[index] + TIME_STEP * rate)
            if stage:
                result = keep * flow[0, index].reshape(8, 8, 128) + result
            if stage < 2:
                flow[stage + 1, index] = result.reshape(64, 128)
            else:
                flow_out[index] = result
        if stage < 2:
            pack_halos(stage + 1)
            halos.append(halo_copies(stage + 1))
            for copy in halos[-1]:
                copy.start()
        inverse = 1.0 / fields[0]
        speed = [fields[1 + part] * inverse for part in range(3)]
        curl = [part_y[6] - part_z[6], part_z[5] - part_x[6], part_x[5] - part_y[5]]
        lamb = [
            (curl[1] * speed[2] - curl[2] * speed[1]).reshape(64, 128),
            (curl[2] * speed[0] - curl[0] * speed[2]).reshape(64, 128),
            (curl[0] * speed[1] - curl[1] * speed[0]).reshape(64, 128),
        ]
        modes = dot(pair_ref[...], jnp.concatenate(lamb, 1))
        empty = jnp.zeros((64, 128), F32)
        doubled = []
        for part in range(3):
            piece = modes[:, 128 * part : 128 * part + 128]
            doubled.append(jnp.concatenate([piece, empty], 1))
            doubled.append(jnp.concatenate([empty, piece], 1))
        routed = dot_nt(route_ref[...], jnp.concatenate(doubled, 0))
        for part in range(3):
            packed[stage, :, part] = routed[:, 128 * part : 128 * part + 128].reshape(n_y, 8, 128)

    def own_rate(stage):
        state = sound[stage]
        mixed = dot(slope_ref[...], jnp.concatenate([state[0], state[1], state[2]], 1))
        depth = dot(jnp.concatenate([state[0], state[3]], 0), slope_z_ref[...])
        rate_ref[0] = -squared * (mixed[:64, 128:256] + mixed[64:, 256:] + depth[64:])
        rate_ref[1] = -mixed[:64, :128]
        rate_ref[2] = -mixed[64:, :128]
        rate_ref[3] = -depth[:64]
        for copy in traces[stage]:
            copy.wait_recv()
        jumps = []
        for face in range(6):
            axis, upper = face // 2, face % 2
            if upper:
                sides = [trace[stage, 0, axis], trace_recv[stage, 1, axis]]
            else:
                sides = [trace_recv[stage, 0, axis], trace[stage, 1, axis]]
            found = pick(
                jnp.concatenate([side.reshape(32, 128) for side in sides], 1), gather_ref[face]
            )
            jumps.append(PENALTY * (found.reshape(4, 8, 128) - trace[stage, upper, axis]))
        rate_ref[:, 0:8, :] += jumps[0]
        rate_ref[:, 56:64, :] += jumps[1]
        rate_ref[:, pl.ds(0, 8, stride=8), :] += jumps[2]
        rate_ref[:, pl.ds(7, 8, stride=8), :] += jumps[3]
        for x in range(8):
            low = pltpu.roll(jumps[4], 128 - x, 2) if x else jumps[4]
            high = pltpu.roll(jumps[5], 7 - x, 2) if x < 7 else jumps[5]
            rate_ref[:, 8 * x : 8 * x + 8, :] += jnp.where(
                digit == 0, low, jnp.where(digit == 7, high, 0.0)
            )

    def add_sources(stage):
        spread_whole(*packet_args(stage)).wait_recv()
        pieces = []
        for part in range(3):
            across = arrived[stage, :, part].reshape(rows_out, 128).T
            pieces.append(jnp.concatenate([across[:64], across[64:]], 1))
        source = pick(jnp.concatenate(pieces, 0), place_ref[...])
        keep, scale = BLEND[stage]
        results = []
        for field in range(4):
            rate = rate_ref[field]
            if field:
                rate = rate + source[64 * (field - 1) : 64 * field]
            result = scale * (sound[stage, field] + TIME_STEP * rate)
            if stage:
                result = keep * sound[0, field] + result
            results.append(result)
        return results

    def next_sound(stage):
        for field, result in enumerate(add_sources(stage)):
            sound[stage + 1, field] = result
        take_traces(stage + 1)
        traces.append(trace_copies(stage + 1))
        for copy in traces[-1]:
            copy.start()

    flow_stage(0)
    spread(packet_args(0))
    keep_own(packet_args(0))

    spread_whole(*label_args()).wait_recv()
    come = labels_recv[...].reshape(rows_out, 128)
    wanted = (eighth(column) + 1).astype(F32)
    for slot in range(2):
        place_ref[slot * rows_out : (slot + 1) * rows_out, :] = (
            (same_digit & (come[:, 64 * slot : 64 * slot + 1] == wanted)).astype(F32).astype(BF16)
        )
    own_rate(0)

    flow_stage(1)
    spread(packet_args(1))
    keep_own(packet_args(1))
    next_sound(0)
    flow_stage(2)
    spread(packet_args(2), 0, 6)
    keep_own(packet_args(2))
    own_rate(1)
    spread(packet_args(2), 6)
    next_sound(1)
    own_rate(2)
    final = swap_groups(jnp.concatenate(add_sources(2), 0).reshape(16, 16, 128))
    for field in range(4):
        for part in range(4):
            sound_out[:, field, 128 * part : 128 * part + 128] = final[4 * field + part]

    for stage in range(3):
        for copy in halos[stage] + traces[stage]:
            copy.wait_send()
        spread_whole(*packet_args(stage)).wait_send()
    spread_whole(*label_args()).wait_send()


def hand_over(flow_in, sound_in, flow_result, sound_result, sem):
    copies = [
        pltpu.make_async_copy(flow_in, flow_result, sem.at[0]),
        pltpu.make_async_copy(sound_in, sound_result, sem.at[1]),
    ]
    for copy in copies:
        copy.start()
    for copy in copies:
        copy.wait()


def solution(mesh):
    sizes = (mesh.shape["fx"], mesh.shape["fy"], mesh.shape["fz"])
    n_y = sizes[1]

    def per_device(
        density,
        velocity,
        pressure,
        acoustic,
        sound_speed,
        derivative,
        mode_basis,
        neighbours,
        block_owner,
        block_element,
    ):
        vmem, hbm = pl.BlockSpec(memory_space=pltpu.VMEM), pl.BlockSpec(memory_space=pltpu.HBM)
        results = (
            jax.ShapeDtypeStruct((5, 8, 8, 128), F32),
            jax.ShapeDtypeStruct((16, 4, 512), F32),
        )
        states = pl.pallas_call(
            functools.partial(kernel, sizes),
            out_shape=results,
            in_specs=[hbm] * 10,
            out_specs=(vmem, vmem),
            scratch_shapes=[
                pltpu.VMEM((3, 5, 64, 128), F32),
                pltpu.VMEM((3, 4, 5, 8, 128), F32),
                pltpu.VMEM((3, 6, 5, 8, 128), F32),
                pltpu.VMEM((7, 64, 128), F32),
                pltpu.VMEM((3, 4, 64, 128), F32),
                pltpu.VMEM((3, 2, 3, 4, 8, 128), F32),
                pltpu.VMEM((3, 2, 3, 4, 8, 128), F32),
                pltpu.VMEM((4, 64, 128), F32),
                pltpu.VMEM((3, n_y, 3, 8, 128), F32),
                pltpu.VMEM((3, n_y, 3, 8, 128), F32),
                pltpu.VMEM((n_y, 8, 128), F32),
                pltpu.VMEM((n_y, 8, 128), F32),
                pltpu.VMEM((6, 256, 128), BF16),
                pltpu.VMEM((16 * n_y, 128), BF16),
                pltpu.VMEM((8 * n_y, 256), F32),
                pltpu.VMEM((64, 64), F32),
                pltpu.VMEM((128, 64), F32),
                pltpu.VMEM((128, 128), F32),
                pltpu.SemaphoreType.DMA((3, 6)),
                pltpu.SemaphoreType.DMA((3, 6)),
                pltpu.SemaphoreType.DMA((3, 2)),
                pltpu.SemaphoreType.DMA((3, 2)),
                pltpu.SemaphoreType.DMA((3,)),
                pltpu.SemaphoreType.DMA((3,)),
                pltpu.SemaphoreType.DMA((1,)),
                pltpu.SemaphoreType.DMA((1,)),
                pltpu.VMEM((8, 8, 128), F32),
                pltpu.VMEM((3, 8, 8, 128), F32),
                pltpu.VMEM((8, 8, 128), F32),
                pltpu.VMEM((16, 4, 512), F32),
                pltpu.VMEM((1, 16), F32),
                pltpu.VMEM((8, 8), F32),
                pltpu.VMEM((8, 8), F32),
                pltpu.VMEM((6, 16), jnp.int32),
                pltpu.VMEM((1, 16), jnp.int32),
                pltpu.VMEM((1, 16), jnp.int32),
                pltpu.SemaphoreType.DMA((10,)),
            ],
            compiler_params=pltpu.CompilerParams(
                collective_id=0, has_side_effects=True, vmem_limit_bytes=40 * 1024 * 1024
            ),
            name="step",
        )(
            *(
                pltpu.with_memory_space_constraint(value, pltpu.HBM)
                for value in (
                    density,
                    velocity,
                    pressure,
                    acoustic,
                    sound_speed.reshape(1, 16),
                    derivative,
                    mode_basis,
                    neighbours.T,
                    block_owner.reshape(1, 16),
                    block_element.reshape(1, 16),
                )
            )
        )
        return pl.pallas_call(
            hand_over,
            out_shape=results,
            in_specs=[vmem, vmem],
            out_specs=(hbm, hbm),
            scratch_shapes=[pltpu.SemaphoreType.DMA((2,))],
            compiler_params=pltpu.CompilerParams(vmem_limit_bytes=40 * 1024 * 1024),
            name="hand_over",
        )(*states)

    placed = (
        P("fx", "fy", "fz"),
        P(None, "fx", "fy", "fz"),
        P("fx", "fy", "fz"),
        P(("fx", "fy", "fz"), None, None),
        P(("fx", "fy", "fz")),
        P(),
        P(),
        P(("fx", "fy", "fz"), None),
        P("fx", "fy", "fz", None, None),
        P("fx", "fy", "fz", None),
    )
    return jax.shard_map(
        per_device,
        mesh=mesh,
        in_specs=placed,
        out_specs=(P(None, "fx", "fy", "fz"), P(("fx", "fy", "fz"), None, None)),
        check_vma=False,
    )
```

```python
import functools

import jax
import jax.numpy as jnp
from jax import lax
from jax.experimental import pallas as pl
from jax.experimental.pallas import tpu as pltpu
from jax.sharding import PartitionSpec as P

HEAT_RATIO = 1.4
TIME_STEP = 0.1
VISCOSITY = 0.05
PENALTY = 0.5
HIGHEST = lax.Precision.HIGHEST
MESH = pl.DeviceIdType.MESH
BLEND = ((0.0, 1.0), (0.75, 0.25), (1.0 / 3.0, 2.0 / 3.0))
F32 = jnp.float32
BF16 = jnp.bfloat16


def dot(a, b):
    return jnp.dot(a, b, precision=HIGHEST, preferred_element_type=F32)


def dot_nt(a, b):
    return lax.dot_general(
        a, b, (((1,), (1,)), ((), ())), precision=HIGHEST, preferred_element_type=F32
    )


def pick(values, chooser):
    rows = values.shape[0]
    high = values.astype(BF16)
    rest = values - high.astype(F32)
    middle = rest.astype(BF16)
    low = (rest - middle.astype(F32)).astype(BF16)
    parts = jnp.dot(
        jnp.concatenate([high, middle, low], 0), chooser, preferred_element_type=F32
    )
    return parts[:rows] + parts[rows : 2 * rows] + parts[2 * rows :]


def iota(shape, dim):
    return lax.broadcasted_iota(jnp.int32, shape, dim)


def eighth(values):
    return lax.shift_right_logical(values, 3)


def repeat_rows(matrix, count, by_block, turned=False):
    rows, columns = iota((count, 8), 0), iota((count, 8), 1)
    chooser = ((eighth(rows) if by_block else rows & 7) == columns).astype(F32)
    if turned:
        return dot_nt(chooser, dot(chooser, matrix))
    return dot_nt(dot(chooser, matrix), chooser)


def swap_groups(values):
    rows, groups = iota((16, 128), 0), eighth(iota((16, 128), 1))
    for bit in range(4):
        step = 1 << bit
        row_bit, group_bit = (rows & step) != 0, (groups & step) != 0
        down = pltpu.roll(pltpu.roll(values, 16 - step, 1), 8 * step, 2)
        up = pltpu.roll(pltpu.roll(values, step, 1), 128 - 8 * step, 2)
        values = jnp.where(
            (row_bit == group_bit)[None], values, jnp.where(group_bit[None], down, up)
        )
    return values


def sweep(cells, along):
    density, momentum, energy = cells[0], cells[1:4], cells[4]
    inverse = 1.0 / density
    velocity = [part * inverse for part in momentum]
    kinetic = sum(part * speed for part, speed in zip(momentum, velocity))
    pressure = (HEAT_RATIO - 1.0) * (energy - 0.5 * kinetic)
    normal = velocity[along]
    signal = jnp.abs(normal) + jnp.sqrt(HEAT_RATIO * jnp.abs(pressure) * inverse)
    half_speed = 0.5 * jnp.maximum(signal[:-1], signal[1:])
    fluxes = [momentum[along]] + [part * normal for part in momentum] + [(energy + pressure) * normal]
    fluxes[1 + along] = fluxes[1 + along] + pressure
    rates = []
    for index, (flux, cell) in enumerate(zip(fluxes, cells)):
        gap = cell[1:] - cell[:-1]
        face = 0.5 * (flux[:-1] + flux[1:]) - half_speed * gap
        rate = face[:-1] - face[1:]
        if 1 <= index <= 3:
            rate = rate + VISCOSITY * (gap[1:] - gap[:-1])
        rates.append(rate)
    slopes = [0.5 * (velocity[c][2:] - velocity[c][:-2]) for c in range(3) if c != along]
    return rates + slopes


def kernel(
    sizes,
    density_in,
    velocity_in,
    pressure_in,
    acoustic_in,
    speed_in,
    derivative_in,
    basis_in,
    neighbour_in,
    owner_in,
    element_in,
    flow_out,
    sound_out,
    flow,
    halo_send,
    halo_recv,
    turned,
    sound,
    trace,
    trace_recv,
    rate_ref,
    packed,
    arrived,
    labels,
    labels_recv,
    gather_ref,
    place_ref,
    route_ref,
    pair_ref,
    slope_ref,
    slope_z_ref,
    halo_out_sem,
    halo_in_sem,
    trace_out_sem,
    trace_in_sem,
    packed_out_sem,
    packed_in_sem,
    label_out_sem,
    label_in_sem,
    density_ref,
    velocity_ref,
    pressure_ref,
    acoustic_ref,
    speed_ref,
    derivative_ref,
    basis_ref,
    neighbour_ref,
    owner_ref,
    element_ref,
    load_sem,
):
    n_x, n_y, n_z = sizes
    fx, fy, fz = lax.axis_index("fx"), lax.axis_index("fy"), lax.axis_index("fz")
    place = (fx * n_y + fy) * n_z + fz
    total = n_x * n_y * n_z

    def device_at(index):
        return (index // (n_y * n_z), (index // n_z) % n_y, index % n_z)

    after, before = device_at((place + 1) % total), device_at((place + total - 1) % total)
    beside = [
        ((fx + 1) % n_x, fy, fz),
        ((fx + n_x - 1) % n_x, fy, fz),
        (fx, (fy + 1) % n_y, fz),
        (fx, (fy + n_y - 1) % n_y, fz),
        (fx, fy, (fz + 1) % n_z),
        (fx, fy, (fz + n_z - 1) % n_z),
    ]
    barrier = pltpu.get_barrier_semaphore()
    for device in [beside[0], beside[1], beside[4], beside[5], after, before]:
        pl.semaphore_signal(barrier, inc=1, device_id=device, device_id_type=MESH)

    @pl.loop(1, n_y)
    def _(step):
        pl.semaphore_signal(
            barrier, inc=1, device_id=(fx, (fy + step) % n_y, fz), device_id_type=MESH
        )

    loads = [
        pltpu.make_async_copy(source, target, load_sem.at[index])
        for index, (source, target) in enumerate(
            (
                (velocity_in, velocity_ref),
                (density_in, density_ref),
                (pressure_in, pressure_ref),
                (acoustic_in, acoustic_ref),
                (owner_in, owner_ref),
                (element_in, element_ref),
                (basis_in, basis_ref),
                (derivative_in, derivative_ref),
                (neighbour_in, neighbour_ref),
                (speed_in, speed_ref),
            )
        )
    ]
    for copy in loads:
        copy.start()

    lane = iota((8, 128), 1)
    digit = lane & 7

    def pack_halos(stage):
        for side, row in ((0, 7), (1, 0)):
            halo_send[stage, side] = flow[stage, :, pl.ds(row, 8, stride=8), :]
        ends = [jnp.zeros((5, 8, 128), F32)] * 2
        for x in range(8):
            plane = flow[stage, :, 8 * x : 8 * x + 8, :]
            ends[0] = jnp.where(lane == x, pltpu.roll(plane, x + 1, 2), ends[0])
            ends[1] = jnp.where(lane == x, pltpu.roll(plane, x, 2) if x else plane, ends[1])
        halo_send[stage, 2], halo_send[stage, 3] = ends

    def halo_copies(stage):
        sources = [flow.at[stage, :, pl.ds(56, 8), :], flow.at[stage, :, pl.ds(0, 8), :]]
        sources += [halo_send.at[stage, index] for index in range(4)]
        return [
            pltpu.make_async_remote_copy(
                src_ref=source,
                dst_ref=halo_recv.at[stage, index],
                send_sem=halo_out_sem.at[stage, index],
                recv_sem=halo_in_sem.at[stage, index],
                device_id=beside[index],
                device_id_type=MESH,
            )
            for index, source in enumerate(sources)
        ]

    def take_traces(stage):
        trace[stage, 0, 0] = sound[stage, :, 0:8, :]
        trace[stage, 1, 0] = sound[stage, :, 56:64, :]
        trace[stage, 0, 1] = sound[stage, :, pl.ds(0, 8, stride=8), :]
        trace[stage, 1, 1] = sound[stage, :, pl.ds(7, 8, stride=8), :]
        ends = [jnp.zeros((4, 8, 128), F32)] * 2
        for x in range(8):
            plane = sound[stage, :, 8 * x : 8 * x + 8, :]
            ends[0] = jnp.where(digit == x, pltpu.roll(plane, x, 2) if x else plane, ends[0])
            ends[1] = jnp.where(digit == x, pltpu.roll(plane, 121 + x, 2) if x < 7 else plane, ends[1])
        trace[stage, 0, 2], trace[stage, 1, 2] = ends

    def trace_copies(stage):
        return [
            pltpu.make_async_remote_copy(
                src_ref=trace.at[stage, 1 - side],
                dst_ref=trace_recv.at[stage, side],
                send_sem=trace_out_sem.at[stage, side],
                recv_sem=trace_in_sem.at[stage, side],
                device_id=device,
                device_id_type=MESH,
            )
            for side, device in ((0, after), (1, before))
        ]

    def spread(args, first=0, last=n_y):
        source, target, out_sem, in_sem = args

        @pl.loop(first, last)
        def _(rank):
            peer = (rank + n_y - 1) % n_y

            @pl.when(peer != fy)
            def _():
                pltpu.make_async_remote_copy(
                    src_ref=source.at[peer],
                    dst_ref=target.at[fy],
                    send_sem=out_sem,
                    recv_sem=in_sem,
                    device_id=(fx, peer, fz),
                    device_id_type=MESH,
                ).start()

    def keep_own(args):
        source, target = args[:2]
        target[fy] = source[fy]

    def spread_whole(source, target, out_sem, in_sem):
        return pltpu.make_async_remote_copy(
            src_ref=source.at[pl.ds(0, n_y - 1)],
            dst_ref=target.at[pl.ds(0, n_y - 1)],
            send_sem=out_sem,
            recv_sem=in_sem,
            device_id=beside[2],
            device_id_type=MESH,
        )

    def label_args():
        return (labels, labels_recv, label_out_sem.at[0], label_in_sem.at[0])

    def packet_args(stage):
        return (
            packed.at[stage],
            arrived.at[stage],
            packed_out_sem.at[stage],
            packed_in_sem.at[stage],
        )

    for copy in loads[:3]:
        copy.wait()
    density = density_ref[...].reshape(64, 128)
    speeds = velocity_ref[...].reshape(3, 64, 128)
    energy = pressure_ref[...].reshape(64, 128) / (HEAT_RATIO - 1.0) + 0.5 * density * (
        speeds[0] * speeds[0] + speeds[1] * speeds[1] + speeds[2] * speeds[2]
    )
    flow[0, 0] = density
    for part in range(3):
        flow[0, 1 + part] = density * speeds[part]
    flow[0, 4] = energy
    pack_halos(0)

    pl.semaphore_wait(barrier, 6 + n_y - 1)
    halos = [halo_copies(0)]
    for copy in halos[0]:
        copy.start()

    for copy in loads[3:]:
        copy.wait()
    nodes = jnp.stack(
        [
            acoustic_ref[:, field, 128 * part : 128 * part + 128]
            for field in range(4)
            for part in range(4)
        ],
        0,
    )
    sound[0] = swap_groups(nodes).reshape(4, 64, 128)
    take_traces(0)
    traces = [trace_copies(0)]
    for copy in traces[0]:
        copy.start()

    widen = (iota((16, 128), 0) == eighth(iota((16, 128), 1))).astype(F32)
    owner = dot(owner_ref[...].astype(F32), widen)
    element = dot(element_ref[...].astype(F32), widen)
    rows_out = 8 * n_y
    row, column = iota((rows_out, 128), 0), iota((rows_out, 128), 1)
    same_digit = (row & 7) == (column & 7)
    earlier = (
        (eighth(iota((128, 128), 0)) < eighth(iota((128, 128), 1)))
        & ((iota((128, 128), 0) & 7) == 0)
    ).astype(F32)
    named = owner.astype(jnp.int32) == eighth(row)
    count = jnp.dot(named.astype(BF16), earlier.astype(BF16), preferred_element_type=F32)
    first, second = named & (count < 0.5), named & (count > 0.5)
    mark = jnp.where((column & 7) == 0, element + 1.0, 0.0)
    label = jnp.where(
        column < 64,
        jnp.sum(jnp.where(first, mark, 0.0), 1, keepdims=True),
        jnp.sum(jnp.where(second, mark, 0.0), 1, keepdims=True),
    )
    labels[...] = label.reshape(n_y, 8, 128)
    spread(label_args())
    keep_own(label_args())

    basis = basis_ref[...]
    tiled = repeat_rows(basis, 128, False)[:rows_out]
    route_ref[:, 0:128] = jnp.where(first, tiled, 0.0)
    route_ref[:, 128:256] = jnp.where(second, tiled, 0.0)
    pair_ref[...] = repeat_rows(basis, 64, True) * repeat_rows(basis, 64, False)

    derivative = derivative_ref[...]
    row64, column64 = iota((64, 64), 0), iota((64, 64), 1)
    slope_ref[0:64, :] = jnp.where(
        (row64 & 7) == (column64 & 7), repeat_rows(derivative, 64, True), 0.0
    )
    slope_ref[64:128, :] = jnp.where(
        eighth(row64) == eighth(column64), repeat_rows(derivative, 64, False), 0.0
    )
    row128, column128 = iota((128, 128), 0), iota((128, 128), 1)
    slope_z_ref[...] = jnp.where(
        eighth(row128) == eighth(column128), repeat_rows(derivative, 128, False, True), 0.0
    )

    local = (neighbour_ref[...] - place * 16).astype(F32)
    nearby = dot(local, widen).astype(jnp.int32)
    row256, column256 = iota((256, 128), 0), iota((256, 128), 1)
    matching = (row256 & 7) == (column256 & 7)
    for face in range(6):
        index = nearby[face : face + 1] + (16 if face % 2 == 0 else 0)
        gather_ref[face] = (matching & (eighth(row256) == index)).astype(F32).astype(BF16)

    squared = dot(speed_ref[...], widen)
    squared = squared * squared

    def flow_stage(stage):
        for copy in halos[stage]:
            copy.wait_recv()
        fields = flow[stage].reshape(5, 8, 8, 128)
        along_x = jnp.concatenate(
            [halo_recv[stage, 0][:, None], fields, halo_recv[stage, 1][:, None]], 1
        )
        part_x = sweep(along_x, 0)
        along_y = jnp.stack(
            [halo_recv[stage, 2]]
            + [flow[stage, :, pl.ds(y, 8, stride=8), :] for y in range(8)]
            + [halo_recv[stage, 3]],
            1,
        )
        part_y = jnp.stack(sweep(along_y, 1), 0)
        for y in range(8):
            turned[:, pl.ds(y, 8, stride=8), :] = part_y[:, y]
        low, high = (
            jnp.stack(
                [
                    jnp.broadcast_to(halo_recv[stage, side][:, :, x : x + 1], (5, 8, 128))
                    for x in range(8)
                ],
                1,
            )
            for side in (4, 5)
        )
        below = jnp.where(lane == 0, low, pltpu.roll(fields, 1, 3))
        above = jnp.where(lane == 127, high, pltpu.roll(fields, 127, 3))
        part_z = [part[0] for part in sweep(jnp.stack([below, fields, above], 1), 2)]
        part_y = [turned[index].reshape(8, 8, 128) for index in range(7)]
        keep, scale = BLEND[stage]
        for index in range(5):
            rate = part_x[index] + part_y[index] + part_z[index]
            result = scale * (fields[index] + TIME_STEP * rate)
            if stage:
                result = keep * flow[0, index].reshape(8, 8, 128) + result
            if stage < 2:
                flow[stage + 1, index] = result.reshape(64, 128)
            else:
                flow_out[index] = result
        if stage < 2:
            pack_halos(stage + 1)
            halos.append(halo_copies(stage + 1))
            for copy in halos[-1]:
                copy.start()
        inverse = 1.0 / fields[0]
        speed = [fields[1 + part] * inverse for part in range(3)]
        curl = [part_y[6] - part_z[6], part_z[5] - part_x[6], part_x[5] - part_y[5]]
        lamb = [
            (curl[1] * speed[2] - curl[2] * speed[1]).reshape(64, 128),
            (curl[2] * speed[0] - curl[0] * speed[2]).reshape(64, 128),
            (curl[0] * speed[1] - curl[1] * speed[0]).reshape(64, 128),
        ]
        modes = dot(pair_ref[...], jnp.concatenate(lamb, 1))
        empty = jnp.zeros((64, 128), F32)
        doubled = []
        for part in range(3):
            piece = modes[:, 128 * part : 128 * part + 128]
            doubled.append(jnp.concatenate([piece, empty], 1))
            doubled.append(jnp.concatenate([empty, piece], 1))
        routed = dot_nt(route_ref[...], jnp.concatenate(doubled, 0))
        for part in range(3):
            packed[stage, :, part] = routed[:, 128 * part : 128 * part + 128].reshape(n_y, 8, 128)

    def own_rate(stage):
        state = sound[stage]
        mixed = dot(slope_ref[...], jnp.concatenate([state[0], state[1], state[2]], 1))
        depth = dot(jnp.concatenate([state[0], state[3]], 0), slope_z_ref[...])
        rate_ref[0] = -squared * (mixed[:64, 128:256] + mixed[64:, 256:] + depth[64:])
        rate_ref[1] = -mixed[:64, :128]
        rate_ref[2] = -mixed[64:, :128]
        rate_ref[3] = -depth[:64]
        for copy in traces[stage]:
            copy.wait_recv()
        jumps = []
        for face in range(6):
            axis, upper = face // 2, face % 2
            if upper:
                sides = [trace[stage, 0, axis], trace_recv[stage, 1, axis]]
            else:
                sides = [trace_recv[stage, 0, axis], trace[stage, 1, axis]]
            found = pick(
                jnp.concatenate([side.reshape(32, 128) for side in sides], 1), gather_ref[face]
            )
            jumps.append(PENALTY * (found.reshape(4, 8, 128) - trace[stage, upper, axis]))
        rate_ref[:, 0:8, :] += jumps[0]
        rate_ref[:, 56:64, :] += jumps[1]
        rate_ref[:, pl.ds(0, 8, stride=8), :] += jumps[2]
        rate_ref[:, pl.ds(7, 8, stride=8), :] += jumps[3]
        for x in range(8):
            low = pltpu.roll(jumps[4], 128 - x, 2) if x else jumps[4]
            high = pltpu.roll(jumps[5], 7 - x, 2) if x < 7 else jumps[5]
            rate_ref[:, 8 * x : 8 * x + 8, :] += jnp.where(
                digit == 0, low, jnp.where(digit == 7, high, 0.0)
            )

    def add_sources(stage):
        spread_whole(*packet_args(stage)).wait_recv()
        pieces = []
        for part in range(3):
            across = arrived[stage, :, part].reshape(rows_out, 128).T
            pieces.append(jnp.concatenate([across[:64], across[64:]], 1))
        source = pick(jnp.concatenate(pieces, 0), place_ref[...])
        keep, scale = BLEND[stage]
        results = []
        for field in range(4):
            rate = rate_ref[field]
            if field:
                rate = rate + source[64 * (field - 1) : 64 * field]
            result = scale * (sound[stage, field] + TIME_STEP * rate)
            if stage:
                result = keep * sound[0, field] + result
            results.append(result)
        return results

    def next_sound(stage):
        for field, result in enumerate(add_sources(stage)):
            sound[stage + 1, field] = result
        take_traces(stage + 1)
        traces.append(trace_copies(stage + 1))
        for copy in traces[-1]:
            copy.start()

    flow_stage(0)
    spread(packet_args(0))
    keep_own(packet_args(0))

    spread_whole(*label_args()).wait_recv()
    come = labels_recv[...].reshape(rows_out, 128)
    wanted = (eighth(column) + 1).astype(F32)
    for slot in range(2):
        place_ref[slot * rows_out : (slot + 1) * rows_out, :] = (
            (same_digit & (come[:, 64 * slot : 64 * slot + 1] == wanted)).astype(F32).astype(BF16)
        )
    own_rate(0)

    crossing = (fz == 0) | (fz == n_z - 1)
    inner = (fz != 0) & (fz != n_z - 1)
    flow_stage(1)

    spread(packet_args(1), 0, 3)

    @pl.when(crossing)
    def _():
        spread(packet_args(1), 3)

    keep_own(packet_args(1))
    next_sound(0)

    @pl.when(inner)
    def _():
        spread(packet_args(1), 3)

    flow_stage(2)
    spread(packet_args(2), 0, 6)
    keep_own(packet_args(2))
    own_rate(1)
    spread(packet_args(2), 6)
    next_sound(1)
    own_rate(2)
    final = swap_groups(jnp.concatenate(add_sources(2), 0).reshape(16, 16, 128))
    for field in range(4):
        for part in range(4):
            sound_out[:, field, 128 * part : 128 * part + 128] = final[4 * field + part]

    for stage in range(3):
        for copy in halos[stage] + traces[stage]:
            copy.wait_send()
        spread_whole(*packet_args(stage)).wait_send()
    spread_whole(*label_args()).wait_send()


def hand_over(flow_in, sound_in, flow_result, sound_result, sem):
    copies = [
        pltpu.make_async_copy(flow_in, flow_result, sem.at[0]),
        pltpu.make_async_copy(sound_in, sound_result, sem.at[1]),
    ]
    for copy in copies:
        copy.start()
    for copy in copies:
        copy.wait()


def solution(mesh):
    sizes = (mesh.shape["fx"], mesh.shape["fy"], mesh.shape["fz"])
    n_y = sizes[1]

    def per_device(
        density,
        velocity,
        pressure,
        acoustic,
        sound_speed,
        derivative,
        mode_basis,
        neighbours,
        block_owner,
        block_element,
    ):
        vmem, hbm = pl.BlockSpec(memory_space=pltpu.VMEM), pl.BlockSpec(memory_space=pltpu.HBM)
        results = (
            jax.ShapeDtypeStruct((5, 8, 8, 128), F32),
            jax.ShapeDtypeStruct((16, 4, 512), F32),
        )
        states = pl.pallas_call(
            functools.partial(kernel, sizes),
            out_shape=results,
            in_specs=[hbm] * 10,
            out_specs=(vmem, vmem),
            scratch_shapes=[
                pltpu.VMEM((3, 5, 64, 128), F32),
                pltpu.VMEM((3, 4, 5, 8, 128), F32),
                pltpu.VMEM((3, 6, 5, 8, 128), F32),
                pltpu.VMEM((7, 64, 128), F32),
                pltpu.VMEM((3, 4, 64, 128), F32),
                pltpu.VMEM((3, 2, 3, 4, 8, 128), F32),
                pltpu.VMEM((3, 2, 3, 4, 8, 128), F32),
                pltpu.VMEM((4, 64, 128), F32),
                pltpu.VMEM((3, n_y, 3, 8, 128), F32),
                pltpu.VMEM((3, n_y, 3, 8, 128), F32),
                pltpu.VMEM((n_y, 8, 128), F32),
                pltpu.VMEM((n_y, 8, 128), F32),
                pltpu.VMEM((6, 256, 128), BF16),
                pltpu.VMEM((16 * n_y, 128), BF16),
                pltpu.VMEM((8 * n_y, 256), F32),
                pltpu.VMEM((64, 64), F32),
                pltpu.VMEM((128, 64), F32),
                pltpu.VMEM((128, 128), F32),
                pltpu.SemaphoreType.DMA((3, 6)),
                pltpu.SemaphoreType.DMA((3, 6)),
                pltpu.SemaphoreType.DMA((3, 2)),
                pltpu.SemaphoreType.DMA((3, 2)),
                pltpu.SemaphoreType.DMA((3,)),
                pltpu.SemaphoreType.DMA((3,)),
                pltpu.SemaphoreType.DMA((1,)),
                pltpu.SemaphoreType.DMA((1,)),
                pltpu.VMEM((8, 8, 128), F32),
                pltpu.VMEM((3, 8, 8, 128), F32),
                pltpu.VMEM((8, 8, 128), F32),
                pltpu.VMEM((16, 4, 512), F32),
                pltpu.VMEM((1, 16), F32),
                pltpu.VMEM((8, 8), F32),
                pltpu.VMEM((8, 8), F32),
                pltpu.VMEM((6, 16), jnp.int32),
                pltpu.VMEM((1, 16), jnp.int32),
                pltpu.VMEM((1, 16), jnp.int32),
                pltpu.SemaphoreType.DMA((10,)),
            ],
            compiler_params=pltpu.CompilerParams(
                collective_id=0, has_side_effects=True, vmem_limit_bytes=40 * 1024 * 1024
            ),
            name="step",
        )(
            *(
                pltpu.with_memory_space_constraint(value, pltpu.HBM)
                for value in (
                    density,
                    velocity,
                    pressure,
                    acoustic,
                    sound_speed.reshape(1, 16),
                    derivative,
                    mode_basis,
                    neighbours.T,
                    block_owner.reshape(1, 16),
                    block_element.reshape(1, 16),
                )
            )
        )
        return pl.pallas_call(
            hand_over,
            out_shape=results,
            in_specs=[vmem, vmem],
            out_specs=(hbm, hbm),
            scratch_shapes=[pltpu.SemaphoreType.DMA((2,))],
            compiler_params=pltpu.CompilerParams(vmem_limit_bytes=40 * 1024 * 1024),
            name="hand_over",
        )(*states)

    placed = (
        P("fx", "fy", "fz"),
        P(None, "fx", "fy", "fz"),
        P("fx", "fy", "fz"),
        P(("fx", "fy", "fz"), None, None),
        P(("fx", "fy", "fz")),
        P(),
        P(),
        P(("fx", "fy", "fz"), None),
        P("fx", "fy", "fz", None, None),
        P("fx", "fy", "fz", None),
    )
    return jax.shard_map(
        per_device,
        mesh=mesh,
        in_specs=placed,
        out_specs=(P(None, "fx", "fy", "fz"), P(("fx", "fy", "fz"), None, None)),
        check_vma=False,
    )
```

```python
import functools

import jax
import jax.numpy as jnp
from jax import lax
from jax.experimental import pallas as pl
from jax.experimental.pallas import tpu as pltpu
from jax.sharding import PartitionSpec as P

HEAT_RATIO = 1.4
TIME_STEP = 0.1
VISCOSITY = 0.05
PENALTY = 0.5
HIGHEST = lax.Precision.HIGHEST
MESH = pl.DeviceIdType.MESH
BLEND = ((0.0, 1.0), (0.75, 0.25), (1.0 / 3.0, 2.0 / 3.0))
F32 = jnp.float32
BF16 = jnp.bfloat16


def dot(a, b):
    return jnp.dot(a, b, precision=HIGHEST, preferred_element_type=F32)


def dot_nt(a, b):
    return lax.dot_general(
        a, b, (((1,), (1,)), ((), ())), precision=HIGHEST, preferred_element_type=F32
    )


def pick(values, chooser):
    rows = values.shape[0]
    high = values.astype(BF16)
    rest = values - high.astype(F32)
    middle = rest.astype(BF16)
    low = (rest - middle.astype(F32)).astype(BF16)
    parts = jnp.dot(
        jnp.concatenate([high, middle, low], 0), chooser, preferred_element_type=F32
    )
    return parts[:rows] + parts[rows : 2 * rows] + parts[2 * rows :]


def iota(shape, dim):
    return lax.broadcasted_iota(jnp.int32, shape, dim)


def eighth(values):
    return lax.shift_right_logical(values, 3)


def repeat_rows(matrix, count, by_block, turned=False):
    rows, columns = iota((count, 8), 0), iota((count, 8), 1)
    chooser = ((eighth(rows) if by_block else rows & 7) == columns).astype(F32)
    if turned:
        return dot_nt(chooser, dot(chooser, matrix))
    return dot_nt(dot(chooser, matrix), chooser)


def swap_groups(values):
    rows, groups = iota((16, 128), 0), eighth(iota((16, 128), 1))
    for bit in range(4):
        step = 1 << bit
        row_bit, group_bit = (rows & step) != 0, (groups & step) != 0
        down = pltpu.roll(pltpu.roll(values, 16 - step, 1), 8 * step, 2)
        up = pltpu.roll(pltpu.roll(values, step, 1), 128 - 8 * step, 2)
        values = jnp.where(
            (row_bit == group_bit)[None], values, jnp.where(group_bit[None], down, up)
        )
    return values


def sweep(cells, along):
    density, momentum, energy = cells[0], cells[1:4], cells[4]
    inverse = 1.0 / density
    velocity = [part * inverse for part in momentum]
    kinetic = sum(part * speed for part, speed in zip(momentum, velocity))
    pressure = (HEAT_RATIO - 1.0) * (energy - 0.5 * kinetic)
    normal = velocity[along]
    signal = jnp.abs(normal) + jnp.sqrt(HEAT_RATIO * jnp.abs(pressure) * inverse)
    half_speed = 0.5 * jnp.maximum(signal[:-1], signal[1:])
    fluxes = [momentum[along]] + [part * normal for part in momentum] + [(energy + pressure) * normal]
    fluxes[1 + along] = fluxes[1 + along] + pressure
    rates = []
    for index, (flux, cell) in enumerate(zip(fluxes, cells)):
        gap = cell[1:] - cell[:-1]
        face = 0.5 * (flux[:-1] + flux[1:]) - half_speed * gap
        rate = face[:-1] - face[1:]
        if 1 <= index <= 3:
            rate = rate + VISCOSITY * (gap[1:] - gap[:-1])
        rates.append(rate)
    slopes = [0.5 * (velocity[c][2:] - velocity[c][:-2]) for c in range(3) if c != along]
    return rates + slopes


def kernel(
    sizes,
    density_in,
    velocity_in,
    pressure_in,
    acoustic_in,
    speed_in,
    derivative_in,
    basis_in,
    neighbour_in,
    owner_in,
    element_in,
    flow_out,
    sound_out,
    flow,
    halo_send,
    halo_recv,
    turned,
    sound,
    trace,
    trace_recv,
    rate_ref,
    packed,
    arrived,
    labels,
    labels_recv,
    gather_ref,
    place_ref,
    route_ref,
    pair_ref,
    slope_ref,
    slope_z_ref,
    halo_out_sem,
    halo_in_sem,
    trace_out_sem,
    trace_in_sem,
    packed_out_sem,
    packed_in_sem,
    label_out_sem,
    label_in_sem,
    density_ref,
    velocity_ref,
    pressure_ref,
    acoustic_ref,
    speed_ref,
    derivative_ref,
    basis_ref,
    neighbour_ref,
    owner_ref,
    element_ref,
    load_sem,
):
    n_x, n_y, n_z = sizes
    fx, fy, fz = lax.axis_index("fx"), lax.axis_index("fy"), lax.axis_index("fz")
    place = (fx * n_y + fy) * n_z + fz
    total = n_x * n_y * n_z

    def device_at(index):
        return (index // (n_y * n_z), (index // n_z) % n_y, index % n_z)

    after, before = device_at((place + 1) % total), device_at((place + total - 1) % total)
    beside = [
        ((fx + 1) % n_x, fy, fz),
        ((fx + n_x - 1) % n_x, fy, fz),
        (fx, (fy + 1) % n_y, fz),
        (fx, (fy + n_y - 1) % n_y, fz),
        (fx, fy, (fz + 1) % n_z),
        (fx, fy, (fz + n_z - 1) % n_z),
    ]
    loads = [
        pltpu.make_async_copy(source, target, load_sem.at[index])
        for index, (source, target) in enumerate(
            (
                (velocity_in, velocity_ref),
                (density_in, density_ref),
                (pressure_in, pressure_ref),
                (acoustic_in, acoustic_ref),
                (owner_in, owner_ref),
                (element_in, element_ref),
                (basis_in, basis_ref),
                (derivative_in, derivative_ref),
                (neighbour_in, neighbour_ref),
                (speed_in, speed_ref),
            )
        )
    ]
    for copy in loads:
        copy.start()

    barrier = pltpu.get_barrier_semaphore()
    for device in [beside[0], beside[1], beside[4], beside[5], after, before]:
        pl.semaphore_signal(barrier, inc=1, device_id=device, device_id_type=MESH)

    @pl.loop(1, n_y)
    def _(step):
        pl.semaphore_signal(
            barrier, inc=1, device_id=(fx, (fy + step) % n_y, fz), device_id_type=MESH
        )

    lane = iota((8, 128), 1)
    digit = lane & 7

    def pack_halos(stage):
        for side, row in ((0, 7), (1, 0)):
            halo_send[stage, side] = flow[stage, :, pl.ds(row, 8, stride=8), :]
        ends = [jnp.zeros((5, 8, 128), F32)] * 2
        for x in range(8):
            plane = flow[stage, :, 8 * x : 8 * x + 8, :]
            ends[0] = jnp.where(lane == x, pltpu.roll(plane, x + 1, 2), ends[0])
            ends[1] = jnp.where(lane == x, pltpu.roll(plane, x, 2) if x else plane, ends[1])
        halo_send[stage, 2], halo_send[stage, 3] = ends

    def halo_copies(stage):
        sources = [flow.at[stage, :, pl.ds(56, 8), :], flow.at[stage, :, pl.ds(0, 8), :]]
        sources += [halo_send.at[stage, index] for index in range(4)]
        return [
            pltpu.make_async_remote_copy(
                src_ref=source,
                dst_ref=halo_recv.at[stage, index],
                send_sem=halo_out_sem.at[stage, index],
                recv_sem=halo_in_sem.at[stage, index],
                device_id=beside[index],
                device_id_type=MESH,
            )
            for index, source in enumerate(sources)
        ]

    def take_traces(stage):
        trace[stage, 0, 0] = sound[stage, :, 0:8, :]
        trace[stage, 1, 0] = sound[stage, :, 56:64, :]
        trace[stage, 0, 1] = sound[stage, :, pl.ds(0, 8, stride=8), :]
        trace[stage, 1, 1] = sound[stage, :, pl.ds(7, 8, stride=8), :]
        ends = [jnp.zeros((4, 8, 128), F32)] * 2
        for x in range(8):
            plane = sound[stage, :, 8 * x : 8 * x + 8, :]
            ends[0] = jnp.where(digit == x, pltpu.roll(plane, x, 2) if x else plane, ends[0])
            ends[1] = jnp.where(digit == x, pltpu.roll(plane, 121 + x, 2) if x < 7 else plane, ends[1])
        trace[stage, 0, 2], trace[stage, 1, 2] = ends

    def trace_copies(stage):
        return [
            pltpu.make_async_remote_copy(
                src_ref=trace.at[stage, 1 - side],
                dst_ref=trace_recv.at[stage, side],
                send_sem=trace_out_sem.at[stage, side],
                recv_sem=trace_in_sem.at[stage, side],
                device_id=device,
                device_id_type=MESH,
            )
            for side, device in ((0, after), (1, before))
        ]

    def spread(args, first=0, last=n_y):
        source, target, out_sem, in_sem = args

        @pl.loop(first, last)
        def _(rank):
            peer = (rank + n_y - 1) % n_y

            @pl.when(peer != fy)
            def _():
                pltpu.make_async_remote_copy(
                    src_ref=source.at[peer],
                    dst_ref=target.at[fy],
                    send_sem=out_sem,
                    recv_sem=in_sem,
                    device_id=(fx, peer, fz),
                    device_id_type=MESH,
                ).start()

    def keep_own(args):
        source, target = args[:2]
        target[fy] = source[fy]

    def spread_whole(source, target, out_sem, in_sem):
        return pltpu.make_async_remote_copy(
            src_ref=source.at[pl.ds(0, n_y - 1)],
            dst_ref=target.at[pl.ds(0, n_y - 1)],
            send_sem=out_sem,
            recv_sem=in_sem,
            device_id=beside[2],
            device_id_type=MESH,
        )

    def label_args():
        return (labels, labels_recv, label_out_sem.at[0], label_in_sem.at[0])

    def packet_args(stage):
        return (
            packed.at[stage],
            arrived.at[stage],
            packed_out_sem.at[stage],
            packed_in_sem.at[stage],
        )

    for copy in loads[:3]:
        copy.wait()
    density = density_ref[...].reshape(64, 128)
    speeds = velocity_ref[...].reshape(3, 64, 128)
    energy = pressure_ref[...].reshape(64, 128) / (HEAT_RATIO - 1.0) + 0.5 * density * (
        speeds[0] * speeds[0] + speeds[1] * speeds[1] + speeds[2] * speeds[2]
    )
    flow[0, 0] = density
    for part in range(3):
        flow[0, 1 + part] = density * speeds[part]
    flow[0, 4] = energy
    pack_halos(0)

    pl.semaphore_wait(barrier, 6 + n_y - 1)
    halos = [halo_copies(0)]
    for copy in halos[0]:
        copy.start()

    for copy in loads[3:]:
        copy.wait()
    nodes = jnp.stack(
        [
            acoustic_ref[:, field, 128 * part : 128 * part + 128]
            for field in range(4)
            for part in range(4)
        ],
        0,
    )
    sound[0] = swap_groups(nodes).reshape(4, 64, 128)
    take_traces(0)
    traces = [trace_copies(0)]
    for copy in traces[0]:
        copy.start()

    widen = (iota((16, 128), 0) == eighth(iota((16, 128), 1))).astype(F32)
    owner = dot(owner_ref[...].astype(F32), widen)
    element = dot(element_ref[...].astype(F32), widen)
    rows_out = 8 * n_y
    row, column = iota((rows_out, 128), 0), iota((rows_out, 128), 1)
    same_digit = (row & 7) == (column & 7)
    earlier = (
        (eighth(iota((128, 128), 0)) < eighth(iota((128, 128), 1)))
        & ((iota((128, 128), 0) & 7) == 0)
    ).astype(F32)
    named = owner.astype(jnp.int32) == eighth(row)
    count = jnp.dot(named.astype(BF16), earlier.astype(BF16), preferred_element_type=F32)
    first, second = named & (count < 0.5), named & (count > 0.5)
    mark = jnp.where((column & 7) == 0, element + 1.0, 0.0)
    label = jnp.where(
        column < 64,
        jnp.sum(jnp.where(first, mark, 0.0), 1, keepdims=True),
        jnp.sum(jnp.where(second, mark, 0.0), 1, keepdims=True),
    )
    labels[...] = label.reshape(n_y, 8, 128)
    spread(label_args())
    keep_own(label_args())

    basis = basis_ref[...]
    tiled = repeat_rows(basis, 128, False)[:rows_out]
    route_ref[:, 0:128] = jnp.where(first, tiled, 0.0)
    route_ref[:, 128:256] = jnp.where(second, tiled, 0.0)
    pair_ref[...] = repeat_rows(basis, 64, True) * repeat_rows(basis, 64, False)

    derivative = derivative_ref[...]
    row64, column64 = iota((64, 64), 0), iota((64, 64), 1)
    slope_ref[0:64, :] = jnp.where(
        (row64 & 7) == (column64 & 7), repeat_rows(derivative, 64, True), 0.0
    )
    slope_ref[64:128, :] = jnp.where(
        eighth(row64) == eighth(column64), repeat_rows(derivative, 64, False), 0.0
    )
    row128, column128 = iota((128, 128), 0), iota((128, 128), 1)
    slope_z_ref[...] = jnp.where(
        eighth(row128) == eighth(column128), repeat_rows(derivative, 128, False, True), 0.0
    )

    local = (neighbour_ref[...] - place * 16).astype(F32)
    nearby = dot(local, widen).astype(jnp.int32)
    row256, column256 = iota((256, 128), 0), iota((256, 128), 1)
    matching = (row256 & 7) == (column256 & 7)
    for face in range(6):
        index = nearby[face : face + 1] + (16 if face % 2 == 0 else 0)
        gather_ref[face] = (matching & (eighth(row256) == index)).astype(F32).astype(BF16)

    squared = dot(speed_ref[...], widen)
    squared = squared * squared

    def flow_stage(stage):
        for copy in halos[stage]:
            copy.wait_recv()
        fields = flow[stage].reshape(5, 8, 8, 128)
        along_x = jnp.concatenate(
            [halo_recv[stage, 0][:, None], fields, halo_recv[stage, 1][:, None]], 1
        )
        part_x = sweep(along_x, 0)
        along_y = jnp.stack(
            [halo_recv[stage, 2]]
            + [flow[stage, :, pl.ds(y, 8, stride=8), :] for y in range(8)]
            + [halo_recv[stage, 3]],
            1,
        )
        part_y = jnp.stack(sweep(along_y, 1), 0)
        for y in range(8):
            turned[:, pl.ds(y, 8, stride=8), :] = part_y[:, y]
        low, high = (
            jnp.stack(
                [
                    jnp.broadcast_to(halo_recv[stage, side][:, :, x : x + 1], (5, 8, 128))
                    for x in range(8)
                ],
                1,
            )
            for side in (4, 5)
        )
        below = jnp.where(lane == 0, low, pltpu.roll(fields, 1, 3))
        above = jnp.where(lane == 127, high, pltpu.roll(fields, 127, 3))
        part_z = [part[0] for part in sweep(jnp.stack([below, fields, above], 1), 2)]
        part_y = [turned[index].reshape(8, 8, 128) for index in range(7)]
        keep, scale = BLEND[stage]
        for index in range(5):
            rate = part_x[index] + part_y[index] + part_z[index]
            result = scale * (fields[index] + TIME_STEP * rate)
            if stage:
                result = keep * flow[0, index].reshape(8, 8, 128) + result
            if stage < 2:
                flow[stage + 1, index] = result.reshape(64, 128)
            else:
                flow_out[index] = result
        if stage < 2:
            pack_halos(stage + 1)
            halos.append(halo_copies(stage + 1))
            for copy in halos[-1]:
                copy.start()
        inverse = 1.0 / fields[0]
        speed = [fields[1 + part] * inverse for part in range(3)]
        curl = [part_y[6] - part_z[6], part_z[5] - part_x[6], part_x[5] - part_y[5]]
        lamb = [
            (curl[1] * speed[2] - curl[2] * speed[1]).reshape(64, 128),
            (curl[2] * speed[0] - curl[0] * speed[2]).reshape(64, 128),
            (curl[0] * speed[1] - curl[1] * speed[0]).reshape(64, 128),
        ]
        modes = dot(pair_ref[...], jnp.concatenate(lamb, 1))
        empty = jnp.zeros((64, 128), F32)
        doubled = []
        for part in range(3):
            piece = modes[:, 128 * part : 128 * part + 128]
            doubled.append(jnp.concatenate([piece, empty], 1))
            doubled.append(jnp.concatenate([empty, piece], 1))
        routed = dot_nt(route_ref[...], jnp.concatenate(doubled, 0))
        for part in range(3):
            packed[stage, :, part] = routed[:, 128 * part : 128 * part + 128].reshape(n_y, 8, 128)

    def own_rate(stage):
        state = sound[stage]
        mixed = dot(slope_ref[...], jnp.concatenate([state[0], state[1], state[2]], 1))
        depth = dot(jnp.concatenate([state[0], state[3]], 0), slope_z_ref[...])
        rate_ref[0] = -squared * (mixed[:64, 128:256] + mixed[64:, 256:] + depth[64:])
        rate_ref[1] = -mixed[:64, :128]
        rate_ref[2] = -mixed[64:, :128]
        rate_ref[3] = -depth[:64]
        for copy in traces[stage]:
            copy.wait_recv()
        jumps = []
        for face in range(6):
            axis, upper = face // 2, face % 2
            if upper:
                sides = [trace[stage, 0, axis], trace_recv[stage, 1, axis]]
            else:
                sides = [trace_recv[stage, 0, axis], trace[stage, 1, axis]]
            found = pick(
                jnp.concatenate([side.reshape(32, 128) for side in sides], 1), gather_ref[face]
            )
            jumps.append(PENALTY * (found.reshape(4, 8, 128) - trace[stage, upper, axis]))
        rate_ref[:, 0:8, :] += jumps[0]
        rate_ref[:, 56:64, :] += jumps[1]
        rate_ref[:, pl.ds(0, 8, stride=8), :] += jumps[2]
        rate_ref[:, pl.ds(7, 8, stride=8), :] += jumps[3]
        for x in range(8):
            low = pltpu.roll(jumps[4], 128 - x, 2) if x else jumps[4]
            high = pltpu.roll(jumps[5], 7 - x, 2) if x < 7 else jumps[5]
            rate_ref[:, 8 * x : 8 * x + 8, :] += jnp.where(
                digit == 0, low, jnp.where(digit == 7, high, 0.0)
            )

    def add_sources(stage):
        spread_whole(*packet_args(stage)).wait_recv()
        pieces = []
        for part in range(3):
            across = arrived[stage, :, part].reshape(rows_out, 128).T
            pieces.append(jnp.concatenate([across[:64], across[64:]], 1))
        source = pick(jnp.concatenate(pieces, 0), place_ref[...])
        keep, scale = BLEND[stage]
        results = []
        for field in range(4):
            rate = rate_ref[field]
            if field:
                rate = rate + source[64 * (field - 1) : 64 * field]
            result = scale * (sound[stage, field] + TIME_STEP * rate)
            if stage:
                result = keep * sound[0, field] + result
            results.append(result)
        return results

    def next_sound(stage):
        for field, result in enumerate(add_sources(stage)):
            sound[stage + 1, field] = result
        take_traces(stage + 1)
        traces.append(trace_copies(stage + 1))
        for copy in traces[-1]:
            copy.start()

    flow_stage(0)
    spread(packet_args(0))
    keep_own(packet_args(0))

    spread_whole(*label_args()).wait_recv()
    come = labels_recv[...].reshape(rows_out, 128)
    wanted = (eighth(column) + 1).astype(F32)
    for slot in range(2):
        place_ref[slot * rows_out : (slot + 1) * rows_out, :] = (
            (same_digit & (come[:, 64 * slot : 64 * slot + 1] == wanted)).astype(F32).astype(BF16)
        )
    own_rate(0)

    crossing = (fz == 0) | (fz == n_z - 1)
    inner = (fz != 0) & (fz != n_z - 1)
    flow_stage(1)

    spread(packet_args(1), 0, 3)

    @pl.when(crossing)
    def _():
        spread(packet_args(1), 3)

    keep_own(packet_args(1))
    next_sound(0)

    @pl.when(inner)
    def _():
        spread(packet_args(1), 3)

    flow_stage(2)
    spread(packet_args(2), 0, 6)
    keep_own(packet_args(2))
    own_rate(1)
    spread(packet_args(2), 6)
    next_sound(1)
    own_rate(2)
    final = swap_groups(jnp.concatenate(add_sources(2), 0).reshape(16, 16, 128))
    for field in range(4):
        for part in range(4):
            sound_out[:, field, 128 * part : 128 * part + 128] = final[4 * field + part]

    for stage in range(3):
        for copy in halos[stage] + traces[stage]:
            copy.wait_send()
        spread_whole(*packet_args(stage)).wait_send()
    spread_whole(*label_args()).wait_send()


def hand_over(flow_in, sound_in, flow_result, sound_result, sem):
    copies = [
        pltpu.make_async_copy(flow_in, flow_result, sem.at[0]),
        pltpu.make_async_copy(sound_in, sound_result, sem.at[1]),
    ]
    for copy in copies:
        copy.start()
    for copy in copies:
        copy.wait()


def solution(mesh):
    sizes = (mesh.shape["fx"], mesh.shape["fy"], mesh.shape["fz"])
    n_y = sizes[1]

    def per_device(
        density,
        velocity,
        pressure,
        acoustic,
        sound_speed,
        derivative,
        mode_basis,
        neighbours,
        block_owner,
        block_element,
    ):
        vmem, hbm = pl.BlockSpec(memory_space=pltpu.VMEM), pl.BlockSpec(memory_space=pltpu.HBM)
        results = (
            jax.ShapeDtypeStruct((5, 8, 8, 128), F32),
            jax.ShapeDtypeStruct((16, 4, 512), F32),
        )
        states = pl.pallas_call(
            functools.partial(kernel, sizes),
            out_shape=results,
            in_specs=[hbm] * 10,
            out_specs=(vmem, vmem),
            scratch_shapes=[
                pltpu.VMEM((3, 5, 64, 128), F32),
                pltpu.VMEM((3, 4, 5, 8, 128), F32),
                pltpu.VMEM((3, 6, 5, 8, 128), F32),
                pltpu.VMEM((7, 64, 128), F32),
                pltpu.VMEM((3, 4, 64, 128), F32),
                pltpu.VMEM((3, 2, 3, 4, 8, 128), F32),
                pltpu.VMEM((3, 2, 3, 4, 8, 128), F32),
                pltpu.VMEM((4, 64, 128), F32),
                pltpu.VMEM((3, n_y, 3, 8, 128), F32),
                pltpu.VMEM((3, n_y, 3, 8, 128), F32),
                pltpu.VMEM((n_y, 8, 128), F32),
                pltpu.VMEM((n_y, 8, 128), F32),
                pltpu.VMEM((6, 256, 128), BF16),
                pltpu.VMEM((16 * n_y, 128), BF16),
                pltpu.VMEM((8 * n_y, 256), F32),
                pltpu.VMEM((64, 64), F32),
                pltpu.VMEM((128, 64), F32),
                pltpu.VMEM((128, 128), F32),
                pltpu.SemaphoreType.DMA((3, 6)),
                pltpu.SemaphoreType.DMA((3, 6)),
                pltpu.SemaphoreType.DMA((3, 2)),
                pltpu.SemaphoreType.DMA((3, 2)),
                pltpu.SemaphoreType.DMA((3,)),
                pltpu.SemaphoreType.DMA((3,)),
                pltpu.SemaphoreType.DMA((1,)),
                pltpu.SemaphoreType.DMA((1,)),
                pltpu.VMEM((8, 8, 128), F32),
                pltpu.VMEM((3, 8, 8, 128), F32),
                pltpu.VMEM((8, 8, 128), F32),
                pltpu.VMEM((16, 4, 512), F32),
                pltpu.VMEM((1, 16), F32),
                pltpu.VMEM((8, 8), F32),
                pltpu.VMEM((8, 8), F32),
                pltpu.VMEM((6, 16), jnp.int32),
                pltpu.VMEM((1, 16), jnp.int32),
                pltpu.VMEM((1, 16), jnp.int32),
                pltpu.SemaphoreType.DMA((10,)),
            ],
            compiler_params=pltpu.CompilerParams(
                collective_id=0, has_side_effects=True, vmem_limit_bytes=40 * 1024 * 1024
            ),
            name="step",
        )(
            *(
                pltpu.with_memory_space_constraint(value, pltpu.HBM)
                for value in (
                    density,
                    velocity,
                    pressure,
                    acoustic,
                    sound_speed.reshape(1, 16),
                    derivative,
                    mode_basis,
                    neighbours.T,
                    block_owner.reshape(1, 16),
                    block_element.reshape(1, 16),
                )
            )
        )
        return pl.pallas_call(
            hand_over,
            out_shape=results,
            in_specs=[vmem, vmem],
            out_specs=(hbm, hbm),
            scratch_shapes=[pltpu.SemaphoreType.DMA((2,))],
            compiler_params=pltpu.CompilerParams(vmem_limit_bytes=40 * 1024 * 1024),
            name="hand_over",
        )(*states)

    placed = (
        P("fx", "fy", "fz"),
        P(None, "fx", "fy", "fz"),
        P("fx", "fy", "fz"),
        P(("fx", "fy", "fz"), None, None),
        P(("fx", "fy", "fz")),
        P(),
        P(),
        P(("fx", "fy", "fz"), None),
        P("fx", "fy", "fz", None, None),
        P("fx", "fy", "fz", None),
    )
    return jax.shard_map(
        per_device,
        mesh=mesh,
        in_specs=placed,
        out_specs=(P(None, "fx", "fy", "fz"), P(("fx", "fy", "fz"), None, None)),
        check_vma=False,
    )
```
